128 devices in a mesh: box: 16 (over x, y_lo, core), depth: 8 (over y_hi, z).
Axes of the slice: x: 4, y: 4 (y_hi: 2, y_lo: 2; y = y_hi * 2 + y_lo), z: 4, core: 2. Of those that a mesh axis runs over, the one named last changes fastest.
Arguments:
- positions: float32 [3, 16384, 128], P(None, ('box', 'depth')), may hold values from -0.5 to 0.5
- charges: float32 [2, 16384, 128], P(None, ('box', 'depth')), may hold values from -0.8 to 0.8
- counts: int32 [16384], P(('box', 'depth')), may hold values from 1 to 128
- owners: int32 [16384, 1], P(('box', 'depth')), may hold values from 0 to 127; in each aligned block of 128 rows (0 to 127, 128 to 255, ...) at most 2 rows name the same one
- leaves: int32 [16384], P(('box', 'depth')), may hold values from 0 to 255
- near_lists: int32 [64, 8, 4096], P(None, 'depth', 'box'), may hold values from 0 to 767
- image_lists: int32 [64, 8, 4096], P(None, 'depth', 'box'), may hold values from 0 to 767
- upward: float32 [304, 304], replicated, may hold values from -0.3125 to 0.3125
- child_ops: bfloat16 [304, 2432], replicated, may hold values from -0.125 to 0.125
- direct_ops: bfloat16 [19456, 304], replicated, may hold values from -0.0390625 to 0.0390625
- image_ops: bfloat16 [19456, 304], replicated, may hold values from -0.0390625 to 0.0390625
Outputs:
- potentials: float32 [304, 8, 4096], P(None, 'depth', 'box')
- parents: float32 [304, 8, 512], P(None, 'depth', 'box')
The draws below stay inside these ranges and needn't reach their ends.
Inputs may be any that keep to these rules, and one draw needn't show every extreme that they name: `owners`: no device's 128 blocks name one owner more than 2 times, and some device's blocks name some owner exactly 2 times.
All inputs are finite; a program needn't handle non-finite values.
Results may differ from the reference program's by a relative error of at most 0.0029.
Values may be sent and summed in bfloat16 or wider, within the bound.
A program may use at most 128 MiB of HBM per device.

```python
import math
import jax
import jax.numpy as jnp
import numpy as np
from jax import lax

LEAF_DEV = 256
SRC_BLK = 128
ROWS = 128
GRID = 6
OFFSETS = 64
CHANNELS = 304
CAP = 2
BLOCKS = 16384
LEAF_ROW = 4096
PARENT_ROW = 512
N_BOX = 16
N_DEPTH = 8


def plant(result, stream_key, smallest, largest):
    place = [jax.random.randint(jax.random.fold_in(stream_key, axis), (), 0, length) for axis, length in enumerate(result.shape)]
    main_axis = result.shape.index(max(result.shape))
    neighbour = place[:main_axis] + [(place[main_axis] + 1) % result.shape[main_axis]] + place[main_axis + 1:]
    return result.at[tuple(place)].set(smallest).at[tuple(neighbour)].set(largest)


def levels(own_key, extent, shards, least, largest):
    def one(position, blocks):
        heights = jax.random.uniform(jax.random.fold_in(jax.random.fold_in(own_key, 6), position), (blocks,), jnp.float32, least / len(shards), largest / len(shards))
        return jnp.repeat(jnp.exp(heights), extent[position] // blocks).reshape((-1,) + (1,) * (len(extent) - position - 1))

    factor_of = one(*shards[0])
    for cut in shards[1:]:
        factor_of = factor_of * one(*cut)
    return factor_of


def deal_out(own_key, own, number, rows, count, top, reach, skew):
    sequence = jax.random.permutation(own_key, count)
    packed, usual = portions_of(count, rows * top, reach, skew, True), portions_of(count, rows * top, reach, skew, False)
    places = jnp.arange(count)

    def named(sizes, offset_by):
        used = int((sizes > 0).sum())
        fixed = max(1, used // 4)
        passed = fixed + (places - fixed + offset_by * (used - fixed)) % max(1, count - fixed)
        return jnp.zeros((count,), jnp.int32).at[sequence[jnp.where(places < fixed, places, passed)]].set(jnp.asarray(sizes, jnp.int32))

    sizes = jnp.where(number % 4 == 0, named(packed, number // 4), named(usual, number - number // 4 - 1))
    mixed = jax.random.permutation(jax.random.fold_in(own, 3), count)
    source_of, receiver = mixed[0:count // 2 * 2:2], mixed[1:count // 2 * 2:2]
    room = jnp.minimum(sizes[source_of] - 1, reach - sizes[receiver]) // 2
    room = jnp.where((source_of == sequence[0]) | (receiver == sequence[0]) | (sizes[receiver] == 0), 0, jnp.maximum(room, 0))
    passed = jax.random.randint(jax.random.fold_in(own, 4), (count // 2,), 0, 1 << 20) % (room + 1)
    sizes = sizes.at[source_of].add(-passed).at[receiver].add(passed)
    labels = jnp.searchsorted(jnp.cumsum(sizes), jnp.arange(rows * top), side="right").astype(jnp.int32)
    table = labels.reshape(top, rows).T
    table = table[jax.random.permutation(jax.random.fold_in(own, 1), rows)]
    offset_by = jax.random.randint(jax.random.fold_in(own, 2), (rows, 1), 0, top)
    return jnp.take_along_axis(table, (jnp.arange(top)[None, :] + offset_by) % top, axis=1)


def portions_of(count, total, reach, slope, full):
    loads = [(1 << 20) // math.isqrt(rank ** slope) + 1 for rank in range(1, count + 1)]
    largest = reach if full else min(reach, max(-(-total // count), total * loads[0] // sum(loads)))
    least = 1 if total - largest >= count - 1 else 0
    holding, surplus = [largest] + [least] * (count - 1), total - largest - least * (count - 1)
    while surplus > 0:
        free = [i for i in range(1, count) if holding[i] < largest] or [i for i in range(1, count) if holding[i] < reach]
        whole, left = sum([loads[i] for i in free]), surplus
        for i in free:
            extra = min(reach - holding[i], max(1, left * loads[i] // whole), surplus)
            holding[i] = holding[i] + extra
            surplus = surplus - extra
    return np.array(holding)


def scatter_about(own_key, shape, width, most, cuts=(), kind=jnp.bfloat16):
    values = jax.random.normal(own_key, shape, jnp.float32) * width
    if len(cuts) > 0:
        values = levels(own_key, shape, cuts, -0.22, 0.18) * values
    return jnp.clip(values, min=-most, max=most).astype(kind)


def setup_inputs(seed: int = 0) -> dict:
    splits = jax.random.split(jax.random.key(seed), 12)
    positions = jnp.clip(jax.random.uniform(splits[0], (3, BLOCKS, ROWS), jnp.float32, -0.5, 0.5) * levels(splits[0], (3, BLOCKS, ROWS), ((1, 128),), -0.4, 0.0), -0.5, 0.5)
    charges = scatter_about(splits[1], (2, BLOCKS, ROWS), 0.1, 0.8, ((1, 128),), jnp.float32)
    counts = plant(jax.random.randint(splits[2], (BLOCKS,), 1, ROWS + 1), jax.random.fold_in(splits[2], 1), 1, ROWS).astype(jnp.int32)
    owners_keys = jax.random.split(jax.random.fold_in(splits[3], 1), BLOCKS // SRC_BLK)
    owners_turns = jax.random.permutation(jax.random.fold_in(splits[3], 3), BLOCKS // SRC_BLK)
    owners = jax.vmap(lambda own, number: deal_out(jax.random.fold_in(splits[3], 2), own, number, SRC_BLK, N_BOX * N_DEPTH, 1, CAP, 2))(owners_keys, owners_turns).reshape((BLOCKS, 1))
    leaves = plant(jax.random.randint(splits[4], (BLOCKS,), 0, LEAF_DEV), jax.random.fold_in(splits[4], 1), 0, LEAF_DEV - 1).astype(jnp.int32)
    near_lists = plant(jax.random.randint(splits[5], (OFFSETS, N_DEPTH, LEAF_ROW), 0, 3 * LEAF_DEV), jax.random.fold_in(splits[5], 1), 0, (3 * LEAF_DEV) - 1).astype(jnp.int32)
    image_lists = plant(jax.random.randint(splits[6], (OFFSETS, N_DEPTH, LEAF_ROW), 0, 3 * LEAF_DEV), jax.random.fold_in(splits[6], 1), 0, (3 * LEAF_DEV) - 1).astype(jnp.int32)
    upward = scatter_about(splits[7], (CHANNELS, CHANNELS), CHANNELS ** -0.5, 0.3125, (), jnp.float32)
    child_ops = scatter_about(splits[8], (CHANNELS, 8 * CHANNELS), (8 * CHANNELS) ** -0.5, 0.125)
    direct_ops = scatter_about(splits[9], (OFFSETS * CHANNELS, CHANNELS), (OFFSETS * CHANNELS) ** -0.5, 0.0390625)
    image_ops = scatter_about(splits[10], (OFFSETS * CHANNELS, CHANNELS), (OFFSETS * CHANNELS) ** -0.5, 0.0390625)
    return dict(positions=positions, charges=charges, counts=counts, owners=owners, leaves=leaves, near_lists=near_lists, image_lists=image_lists, upward=upward, child_ops=child_ops, direct_ops=direct_ops, image_ops=image_ops)


wavenumber = 2.0

def surface_points(grid_size):
    indices = np.arange(grid_size)
    lattice = np.stack(np.meshgrid(indices, indices, indices, indexing='ij'), -1).reshape(-1, 3)
    outside = np.any((lattice == 0) | (lattice == grid_size - 1), axis=1)
    middle = (grid_size - 1) / 2.0
    return ((lattice[outside] - middle) * (1.5 / middle)).astype(np.float32)

def block_check(positions, charges):
    points = jnp.asarray(surface_points(GRID)).astype(positions.dtype)
    delta_x = points[:, 0][:, None, None] - positions[0][None]
    delta_y = points[:, 1][:, None, None] - positions[1][None]
    delta_z = points[:, 2][:, None, None] - positions[2][None]
    radius = jnp.sqrt(delta_x * delta_x + delta_y * delta_y + delta_z * delta_z)
    cosine = jnp.cos(wavenumber * radius) / radius
    sine_part = jnp.sin(wavenumber * radius) / radius
    real_part = lax.optimization_barrier(jnp.sum(cosine * charges[0][None] - sine_part * charges[1][None], axis=2))
    imaginary = lax.optimization_barrier(jnp.sum(sine_part * charges[0][None] + cosine * charges[1][None], axis=2))
    return jnp.concatenate([real_part, imaginary], axis=0)

def checks_by_group(positions, charges):
    blocks = positions.shape[1]
    group_size = math.gcd(blocks, 32)
    group_count = blocks // group_size
    place_groups = positions.reshape(3, group_count, group_size, positions.shape[2]).transpose(1, 0, 2, 3)
    charge_groups = charges.reshape(2, group_count, group_size, charges.shape[2]).transpose(1, 0, 2, 3)

    def one_group(grouped):
        return block_check(grouped[0], grouped[1])
    values = lax.map(one_group, (place_groups, charge_groups))
    return values.transpose(1, 0, 2).reshape(values.shape[1], blocks)

def reference(positions, charges, counts, owners, leaves, near_lists, image_lists, upward, child_ops, direct_ops, image_ops):
    live = (jnp.arange(ROWS, dtype=jnp.int32)[None, :] < counts[:, None]).astype(positions.dtype)
    masked = charges * live[None]
    values = checks_by_group(positions, masked)
    column = owners[:, 0] * LEAF_DEV + leaves
    summed = jax.ops.segment_sum(values.T, column, num_segments=N_BOX * N_DEPTH * LEAF_DEV)
    check = summed.reshape(N_BOX, N_DEPTH, LEAF_DEV, CHANNELS).transpose(3, 1, 0, 2).reshape(CHANNELS, N_DEPTH * LEAF_ROW)
    multipole = jnp.dot(upward, check, precision=lax.Precision.HIGHEST).astype(jnp.bfloat16).reshape(CHANNELS, N_DEPTH, LEAF_ROW)
    children = multipole.reshape(CHANNELS, N_DEPTH, PARENT_ROW, 8).transpose(0, 3, 1, 2).reshape(CHANNELS * 8, N_DEPTH * PARENT_ROW)
    parents = jnp.dot(child_ops, children, preferred_element_type=jnp.float32).reshape(CHANNELS, N_DEPTH, PARENT_ROW)
    padded = jnp.pad(multipole, ((0, 0), (0, 0), (LEAF_DEV, LEAF_DEV)))

    def translate_all(operators, lists, mirror):
        wide_ops = operators.astype(jnp.float32)

        def one_device(device):
            slab = device // N_BOX
            box_number = device % N_BOX
            source = N_DEPTH - 1 - slab if mirror else slab
            plane = lax.dynamic_index_in_dim(padded, source.astype(jnp.int32), 1, keepdims=False)
            chosen = lax.dynamic_slice(lists, (jnp.int32(0), slab.astype(jnp.int32), (box_number * LEAF_DEV).astype(jnp.int32)), (OFFSETS, 1, LEAF_DEV))[:, 0, :]
            gathered = jnp.take(plane, chosen + box_number * LEAF_DEV, axis=1).astype(jnp.float32)
            rows = gathered.transpose(2, 1, 0).reshape(LEAF_DEV, OFFSETS * CHANNELS)
            return jnp.dot(rows, wide_ops, preferred_element_type=jnp.float32).T
        results = lax.map(one_device, jnp.arange(N_DEPTH * N_BOX, dtype=jnp.int32))
        return results.reshape(N_DEPTH, N_BOX, CHANNELS, LEAF_DEV).transpose(2, 0, 1, 3).reshape(CHANNELS, N_DEPTH, LEAF_ROW)
    direct = translate_all(direct_ops, near_lists, False)
    reflected = translate_all(image_ops, image_lists, True)
    return (direct + reflected, parents)
```

```python
import functools

import jax
import jax.numpy as jnp
import numpy as np
from jax import lax
from jax.experimental import pallas as pl
from jax.experimental.pallas import tpu as pltpu
from jax.sharding import PartitionSpec as P
from numpy.polynomial import chebyshev, polynomial

GRID = 6
LANES = 384
VM = pl.BlockSpec(memory_space=pltpu.VMEM)
SM = pl.BlockSpec(memory_space=pltpu.SMEM)


def surface_index(grid_size):
    indices = np.arange(grid_size)
    lattice = np.stack(np.meshgrid(indices, indices, indices, indexing="ij"), -1).reshape(-1, 3)
    outside = np.any((lattice == 0) | (lattice == grid_size - 1), axis=1)
    return lattice[outside].astype(np.int32)


def node_coordinates(grid_size):
    middle = (grid_size - 1) / 2.0
    return ((np.arange(grid_size) - middle) * (1.5 / middle)).astype(np.float32)


def series(function, degree):
    fitted = chebyshev.Chebyshev.interpolate(function, degree, domain=[1.0, 12.0])
    return [float(value) for value in fitted.convert(kind=polynomial.Polynomial).coef]


HALF_SINE = series(lambda s: np.sin(np.sqrt(s) / 2) / (np.sqrt(s) / 2), 4)
HALF_COSINE = series(lambda s: np.cos(np.sqrt(s) / 2), 5)


def horner(coefficients, s):
    value = coefficients[-1] * s + coefficients[-2]
    for coefficient in coefficients[-3::-1]:
        value = value * s + coefficient
    return value


def waves(s):
    sine = horner(HALF_SINE, s)
    cosine = horner(HALF_COSINE, s)
    sine = sine * cosine
    cosine = cosine * cosine
    cosine = (cosine + cosine) - 1.0
    twice = cosine + cosine
    return (twice * cosine - 1.0) * lax.rsqrt(s), twice * sine


def pieces(value, count=3):
    terms = []
    for _ in range(count):
        terms.append(value.astype(jnp.bfloat16))
        value = value - terms[-1].astype(jnp.float32)
    return terms


def sources_kernel(capacity, table, positions, charges, counts, owner_row, owner_col, leaves, out, planes, depths, live_charges, values):
    nodes = node_coordinates(GRID)
    blocks, rows = positions.shape[1:]
    x, y, z = positions[0].T, positions[1].T, positions[2].T
    squares = []
    for node in nodes:
        delta = float(node) - y
        squares.append(delta * delta)
    for i, node in enumerate(nodes):
        delta = float(node) - x
        delta = delta * delta
        for j in range(len(nodes)):
            planes[i * len(nodes) + j] = delta + squares[j]
        delta = float(node) - z
        depths[i] = delta * delta
    live = lax.broadcasted_iota(jnp.int32, (rows, blocks), 0) < counts[...]
    for part in range(2):
        live_charges[part] = jnp.where(live, charges[part].T, 0.0)
    points = table.shape[1]
    values[...] = jnp.zeros_like(values)

    def one_point(p, carry):
        plane = table[0, p]
        depth = table[1, p]
        real = imaginary = None
        for chunk in range(rows // 8):
            place = pl.ds(8 * chunk, 8)
            cosine, sine = waves(planes[plane, place, :] + depths[depth, place, :])
            first = live_charges[0, place, :]
            second = live_charges[1, place, :]
            a = cosine * first - sine * second
            b = sine * first + cosine * second
            real = a if real is None else real + a
            imaginary = b if imaginary is None else imaginary + b
        values[pl.ds(p, 1), :] = jnp.sum(real, axis=0, keepdims=True)
        values[pl.ds(points + p, 1), :] = jnp.sum(imaginary, axis=0, keepdims=True)
        return carry

    lax.fori_loop(0, points, one_point, 0)
    values[pl.ds(2 * points, 1), :] = leaves[...].astype(jnp.float32)
    earlier = (owner_row[...] == owner_col[...]) & (
        lax.broadcasted_iota(jnp.int32, (blocks, blocks), 0)
        < lax.broadcasted_iota(jnp.int32, (blocks, blocks), 1)
    )
    rank = jnp.sum(jnp.where(earlier, 1.0, 0.0), axis=0, keepdims=True).astype(jnp.int32)
    slot = owner_row[...] * capacity + rank
    pick = jnp.where(lax.broadcasted_iota(jnp.int32, (out.shape[0], blocks), 0) == slot, 1.0, 0.0)
    pick = pick.astype(jnp.bfloat16)
    total = None
    for piece in pieces(values[...]):
        term = lax.dot_general(pick, piece, (((1,), (1,)), ((), ())), preferred_element_type=jnp.float32)
        total = term if total is None else total + term
    out[...] = total


def routed_sources(positions, charges, counts, owners, leaves, slots, capacity):
    index = surface_index(GRID)
    table = jnp.asarray(np.stack([index[:, 0] * GRID + index[:, 1], index[:, 2]]))
    blocks, rows = positions.shape[1:]
    return pl.pallas_call(
        functools.partial(sources_kernel, capacity),
        out_shape=jax.ShapeDtypeStruct((slots, LANES), jnp.float32),
        in_specs=[SM] + [VM] * 6,
        out_specs=VM,
        scratch_shapes=[
            pltpu.VMEM((GRID * GRID, rows, blocks), jnp.float32),
            pltpu.VMEM((GRID, rows, blocks), jnp.float32),
            pltpu.VMEM((2, rows, blocks), jnp.float32),
            pltpu.VMEM((LANES, blocks), jnp.float32),
        ],
        compiler_params=pltpu.CompilerParams(vmem_limit_bytes=32 << 20),
        name="sources",
    )(
        table,
        positions,
        charges,
        counts.reshape(1, blocks),
        owners.reshape(1, blocks),
        owners,
        leaves.reshape(1, blocks),
    )


def translate_kernel(batch, lists, windows, direct_ops, image_ops, out, gathered):
    step = pl.program_id(0)
    half = pl.num_programs(0) // 2
    channels = windows.shape[1]
    leaf_count = out.shape[1]
    window = windows[jnp.where(step >= half, 1, 0)]
    row = lax.broadcasted_iota(jnp.int32, (leaf_count, leaf_count), 0)
    for o in range(batch):
        chosen = lists[pl.ds(step * batch + o, 1), :]
        hot = jnp.concatenate(
            [
                jnp.where(row == chosen - part * leaf_count, 1.0, 0.0).astype(jnp.bfloat16)
                for part in range(3)
            ],
            axis=0,
        )
        picked = jnp.dot(window, hot, preferred_element_type=jnp.float32)
        gathered[pl.ds(o * channels, channels), :] = picked.astype(jnp.bfloat16)

    def apply(operators):
        term = jnp.dot(operators[...], gathered[...], preferred_element_type=jnp.float32)

        @pl.when(step == 0)
        def _():
            out[...] = term

        @pl.when(step > 0)
        def _():
            out[...] += term

    @pl.when(step < half)
    def _():
        apply(direct_ops)

    @pl.when(step >= half)
    def _():
        apply(image_ops)


def translate(lists, windows, direct_ops, image_ops):
    channels = windows.shape[1]
    offsets = lists.shape[0] // 2
    leaf_count = lists.shape[1]
    batch = 16
    count = offsets // batch
    return pl.pallas_call(
        functools.partial(translate_kernel, batch),
        out_shape=jax.ShapeDtypeStruct((channels, leaf_count), jnp.float32),
        grid=(2 * count,),
        in_specs=[
            pl.BlockSpec(lists.shape, lambda s: (0, 0)),
            pl.BlockSpec(windows.shape, lambda s: (0, 0, 0)),
            pl.BlockSpec((channels, batch * channels), lambda s: (0, jnp.minimum(s, count - 1))),
            pl.BlockSpec((channels, batch * channels), lambda s: (0, jnp.maximum(s - count, 0))),
        ],
        out_specs=pl.BlockSpec((channels, leaf_count), lambda s: (0, 0)),
        scratch_shapes=[pltpu.VMEM((batch * channels, leaf_count), jnp.bfloat16)],
        compiler_params=pltpu.CompilerParams(vmem_limit_bytes=48 << 20),
        name="translate",
    )(lists, windows, direct_ops, image_ops)


def local(
    positions,
    charges,
    counts,
    owners,
    leaves,
    near_lists,
    image_lists,
    upward,
    child_ops,
    direct_ops,
    image_ops,
):
    box_count = lax.axis_size("box")
    depth_count = lax.axis_size("depth")
    devices = box_count * depth_count
    blocks = positions.shape[1]
    capacity = 2 * blocks // devices
    slots = devices * capacity
    leaf_count = near_lists.shape[2]
    channels = upward.shape[0]
    sent = routed_sources(positions, charges, counts, owners, leaves, slots, capacity)
    arrived = lax.all_to_all(
        sent.reshape(devices, capacity * LANES),
        ("box", "depth"),
        split_axis=0,
        concat_axis=0,
        tiled=True,
    ).reshape(slots, LANES)
    members = (
        arrived[:, channels : channels + 1]
        == jnp.arange(leaf_count, dtype=jnp.float32)[None, :]
    ).astype(jnp.float32)
    raised = lax.dot_general(
        upward, arrived[:, :channels], (((1,), (1,)), ((), ())), precision=lax.Precision.HIGHEST
    )
    multipole = jnp.dot(raised, members, precision=lax.Precision.HIGHEST).astype(jnp.bfloat16)
    children = (
        multipole.reshape(channels, leaf_count // 8, 8)
        .transpose(0, 2, 1)
        .reshape(channels * 8, leaf_count // 8)
    )
    parents = jnp.dot(child_ops, children, preferred_element_type=jnp.float32)

    def routed(shift, mirror):
        pairs = []
        for box in range(box_count):
            for depth in range(depth_count):
                if 0 <= box + shift < box_count:
                    other = depth_count - 1 - depth if mirror else depth
                    pairs.append((box * depth_count + depth, (box + shift) * depth_count + other))
        return lax.ppermute(multipole, ("box", "depth"), pairs)

    windows = jnp.stack(
        [
            jnp.concatenate([routed(1, False), multipole, routed(-1, False)], axis=1),
            jnp.concatenate([routed(1, True), routed(0, True), routed(-1, True)], axis=1),
        ]
    )
    lists = jnp.concatenate([near_lists[:, 0, :], image_lists[:, 0, :]], axis=0)
    potentials = translate(lists, windows, direct_ops.T, image_ops.T)
    return (potentials[:, None, :], parents[:, None, :])


def solution(mesh):
    return jax.shard_map(
        local,
        mesh=mesh,
        in_specs=(
            P(None, ("box", "depth"), None),
            P(None, ("box", "depth"), None),
            P(("box", "depth")),
            P(("box", "depth"), None),
            P(("box", "depth")),
            P(None, "depth", "box"),
            P(None, "depth", "box"),
            P(),
            P(),
            P(),
            P(),
        ),
        out_specs=(P(None, "depth", "box"), P(None, "depth", "box")),
        check_vma=False,
    )
```

```python
import functools

import jax
import jax.numpy as jnp
import numpy as np
from jax import lax
from jax.experimental import pallas as pl
from jax.experimental.pallas import tpu as pltpu
from jax.sharding import PartitionSpec as P
from numpy.polynomial import chebyshev, polynomial

GRID = 6
LANES = 384
VM = pl.BlockSpec(memory_space=pltpu.VMEM)
SM = pl.BlockSpec(memory_space=pltpu.SMEM)


def surface_index(grid_size):
    indices = np.arange(grid_size)
    lattice = np.stack(np.meshgrid(indices, indices, indices, indexing="ij"), -1).reshape(-1, 3)
    outside = np.any((lattice == 0) | (lattice == grid_size - 1), axis=1)
    return lattice[outside].astype(np.int32)


def node_coordinates(grid_size):
    middle = (grid_size - 1) / 2.0
    return ((np.arange(grid_size) - middle) * (1.5 / middle)).astype(np.float32)


def series(function, degree):
    fitted = chebyshev.Chebyshev.interpolate(function, degree, domain=[1.0, 12.0])
    return [float(value) for value in fitted.convert(kind=polynomial.Polynomial).coef]


HALF_SINE = series(lambda s: np.sin(np.sqrt(s) / 2) / (np.sqrt(s) / 2), 4)
HALF_COSINE = series(lambda s: np.cos(np.sqrt(s) / 2), 5)


def horner(coefficients, s):
    value = coefficients[-1] * s + coefficients[-2]
    for coefficient in coefficients[-3::-1]:
        value = value * s + coefficient
    return value


def waves(s):
    sine = horner(HALF_SINE, s)
    cosine = horner(HALF_COSINE, s)
    sine = sine * cosine
    cosine = cosine * cosine
    cosine = (cosine + cosine) - 1.0
    twice = cosine + cosine
    return (twice * cosine - 1.0) * lax.rsqrt(s), twice * sine


def pieces(value, count=3):
    terms = []
    for _ in range(count):
        terms.append(value.astype(jnp.bfloat16))
        value = value - terms[-1].astype(jnp.float32)
    return terms


def sources_kernel(capacity, table, positions, charges, counts, owner_row, owner_col, leaves, out, planes, depths, live_charges, values):
    nodes = node_coordinates(GRID)
    blocks, rows = positions.shape[1:]
    x, y, z = positions[0].T, positions[1].T, positions[2].T
    squares = []
    for node in nodes:
        delta = float(node) - y
        squares.append(delta * delta)
    for i, node in enumerate(nodes):
        delta = float(node) - x
        delta = delta * delta
        for j in range(len(nodes)):
            planes[i * len(nodes) + j] = delta + squares[j]
        delta = float(node) - z
        depths[i] = delta * delta
    live = lax.broadcasted_iota(jnp.int32, (rows, blocks), 0) < counts[...]
    for part in range(2):
        live_charges[part] = jnp.where(live, charges[part].T, 0.0)
    points = table.shape[1]
    values[...] = jnp.zeros_like(values)

    def one_point(p, carry):
        plane = table[0, p]
        depth = table[1, p]
        real = imaginary = None
        for chunk in range(rows // 8):
            place = pl.ds(8 * chunk, 8)
            cosine, sine = waves(planes[plane, place, :] + depths[depth, place, :])
            first = live_charges[0, place, :]
            second = live_charges[1, place, :]
            a = cosine * first - sine * second
            b = sine * first + cosine * second
            real = a if real is None else real + a
            imaginary = b if imaginary is None else imaginary + b
        values[pl.ds(p, 1), :] = jnp.sum(real, axis=0, keepdims=True)
        values[pl.ds(points + p, 1), :] = jnp.sum(imaginary, axis=0, keepdims=True)
        return carry

    lax.fori_loop(0, points, one_point, 0)
    values[pl.ds(2 * points, 1), :] = leaves[...].astype(jnp.float32)
    earlier = (owner_row[...] == owner_col[...]) & (
        lax.broadcasted_iota(jnp.int32, (blocks, blocks), 0)
        < lax.broadcasted_iota(jnp.int32, (blocks, blocks), 1)
    )
    rank = jnp.sum(jnp.where(earlier, 1.0, 0.0), axis=0, keepdims=True).astype(jnp.int32)
    terms = pieces(values[...])
    device = lax.broadcasted_iota(jnp.int32, (out.shape[0], blocks), 0)
    for place in range(capacity):
        pick = jnp.where((device == owner_row[...]) & (rank == place), 1.0, 0.0).astype(jnp.bfloat16)
        out[:, place, :] = sum(
            lax.dot_general(pick, term, (((1,), (1,)), ((), ())), preferred_element_type=jnp.float32)
            for term in terms
        )


def routed_sources(positions, charges, counts, owners, leaves, devices, capacity):
    index = surface_index(GRID)
    table = jnp.asarray(np.stack([index[:, 0] * GRID + index[:, 1], index[:, 2]]))
    blocks, rows = positions.shape[1:]
    return pl.pallas_call(
        functools.partial(sources_kernel, capacity),
        out_shape=jax.ShapeDtypeStruct((devices, capacity, LANES), jnp.float32),
        in_specs=[SM] + [VM] * 6,
        out_specs=VM,
        scratch_shapes=[
            pltpu.VMEM((GRID * GRID, rows, blocks), jnp.float32),
            pltpu.VMEM((GRID, rows, blocks), jnp.float32),
            pltpu.VMEM((2, rows, blocks), jnp.float32),
            pltpu.VMEM((LANES, blocks), jnp.float32),
        ],
        compiler_params=pltpu.CompilerParams(vmem_limit_bytes=32 << 20),
        name="sources",
    )(
        table,
        positions,
        charges,
        counts.reshape(1, blocks),
        owners.reshape(1, blocks),
        owners,
        leaves.reshape(1, blocks),
    )


def exchange_kernel(
    sent, upward, windows, multipole, arrived, send_sem, arrive_sem, halo_send, halo_recv
):
    box, depth = lax.axis_index("box"), lax.axis_index("depth")
    boxes, depths = lax.axis_size("box"), lax.axis_size("depth")
    devices, capacity, _ = sent.shape
    channels, leaf_count = multipole.shape
    me = box * depths + depth

    def route(j, carry):
        target = lax.rem(me + j, devices)
        pltpu.make_async_remote_copy(
            src_ref=sent.at[target],
            dst_ref=arrived.at[me],
            send_sem=send_sem,
            recv_sem=arrive_sem,
            device_id=(target // depths, lax.rem(target, depths)),
            device_id_type=pl.DeviceIdType.MESH,
        ).start()
        return carry

    lax.fori_loop(1, devices, route, 0)
    arrived[me] = sent[me]
    others = pl.ds(0, devices - 1)
    every = pltpu.make_async_remote_copy(
        src_ref=sent.at[others],
        dst_ref=arrived.at[others],
        send_sem=send_sem,
        recv_sem=arrive_sem,
        device_id=(lax.rem(box + 1, boxes), depth),
        device_id_type=pl.DeviceIdType.MESH,
    )
    every.wait_send()
    every.wait_recv()
    values = jnp.concatenate([arrived[:, place, :] for place in range(capacity)], axis=0)
    leaf = values[:, channels : channels + 1].astype(jnp.int32)
    members = jnp.where(
        lax.broadcasted_iota(jnp.int32, (devices * capacity, leaf_count), 1) == leaf, 1.0, 0.0
    ).astype(jnp.bfloat16)
    raised = lax.dot_general(
        upward[...],
        values[:, :channels],
        (((1,), (1,)), ((), ())),
        precision=lax.Precision.HIGHEST,
        preferred_element_type=jnp.float32,
    )
    summed = sum(
        jnp.dot(term, members, preferred_element_type=jnp.float32) for term in pieces(raised)
    )
    own = summed.astype(jnp.bfloat16)
    multipole[...] = own
    windows[0, 1] = own

    def copy(number, source, place, device):
        return pltpu.make_async_remote_copy(
            src_ref=source,
            dst_ref=windows.at[place],
            send_sem=halo_send.at[number],
            recv_sem=halo_recv.at[number],
            device_id=device,
            device_id_type=pl.DeviceIdType.MESH,
        )

    def beside(number, source, slab, device_depth):
        to_right = copy(number, source, (slab, 0), (box + 1, device_depth))
        to_left = copy(number + 1, source, (slab, 2), (box - 1, device_depth))
        return to_right, to_left

    mirror = copy(4, multipole, (1, 1), (box, depths - 1 - depth))
    direct = beside(0, multipole, 0, depth)
    image = beside(2, windows.at[1, 1], 1, depth)
    has_left, has_right = box > 0, box < boxes - 1
    blank = jnp.zeros((channels, leaf_count), jnp.bfloat16)

    mirror.start()

    @pl.when(has_right)
    def _():
        direct[0].start()

    @pl.when(has_left)
    def _():
        direct[1].start()

    @pl.when(jnp.logical_not(has_left))
    def _():
        windows[0, 0] = blank
        windows[1, 0] = blank

    @pl.when(jnp.logical_not(has_right))
    def _():
        windows[0, 2] = blank
        windows[1, 2] = blank

    mirror.wait_recv()

    @pl.when(has_right)
    def _():
        image[0].start()

    @pl.when(has_left)
    def _():
        image[1].start()

    for pair in (direct, image):

        @pl.when(has_left)
        def _():
            pair[0].wait_recv()
            pair[1].wait_send()

        @pl.when(has_right)
        def _():
            pair[1].wait_recv()
            pair[0].wait_send()

    mirror.wait_send()


def exchange(sent, upward, leaf_count):
    channels = upward.shape[0]
    return pl.pallas_call(
        exchange_kernel,
        out_shape=(
            jax.ShapeDtypeStruct((2, 3, channels, leaf_count), jnp.bfloat16),
            jax.ShapeDtypeStruct((channels, leaf_count), jnp.bfloat16),
        ),
        in_specs=[VM, VM],
        out_specs=(VM, VM),
        scratch_shapes=[
            pltpu.VMEM(sent.shape, jnp.float32),
            pltpu.SemaphoreType.DMA,
            pltpu.SemaphoreType.DMA,
            pltpu.SemaphoreType.DMA((5,)),
            pltpu.SemaphoreType.DMA((5,)),
        ],
        compiler_params=pltpu.CompilerParams(vmem_limit_bytes=32 << 20, has_side_effects=True),
        name="exchange",
    )(sent, upward)


def translate_kernel(batch, lists, windows, direct_ops, image_ops, out, gathered):
    step = pl.program_id(0)
    half = pl.num_programs(0) // 2
    channels, leaf_count = out.shape
    slab = jnp.where(step >= half, 1, 0)
    window = jnp.concatenate([windows[slab, part] for part in range(3)], axis=1)
    row = lax.broadcasted_iota(jnp.int32, (leaf_count, leaf_count), 0)
    for o in range(batch):
        chosen = lists[pl.ds(step * batch + o, 1), :]
        hot = jnp.concatenate(
            [
                jnp.where(row == chosen - part * leaf_count, 1.0, 0.0).astype(jnp.bfloat16)
                for part in range(3)
            ],
            axis=0,
        )
        picked = jnp.dot(window, hot, preferred_element_type=jnp.float32)
        gathered[pl.ds(o * channels, channels), :] = picked.astype(jnp.bfloat16)

    def apply(operators):
        term = jnp.dot(operators[...], gathered[...], preferred_element_type=jnp.float32)

        @pl.when(step == 0)
        def _():
            out[...] = term

        @pl.when(step > 0)
        def _():
            out[...] += term

    @pl.when(step < half)
    def _():
        apply(direct_ops)

    @pl.when(step >= half)
    def _():
        apply(image_ops)


def translate(lists, windows, direct_ops, image_ops):
    channels, leaf_count = windows.shape[2:]
    offsets = lists.shape[0] // 2
    batch = 16
    count = offsets // batch
    return pl.pallas_call(
        functools.partial(translate_kernel, batch),
        out_shape=jax.ShapeDtypeStruct((channels, leaf_count), jnp.float32),
        grid=(2 * count,),
        in_specs=[
            pl.BlockSpec(lists.shape, lambda s: (0, 0)),
            pl.BlockSpec(windows.shape, lambda s: (0, 0, 0, 0)),
            pl.BlockSpec((channels, batch * channels), lambda s: (0, jnp.minimum(s, count - 1))),
            pl.BlockSpec((channels, batch * channels), lambda s: (0, jnp.maximum(s - count, 0))),
        ],
        out_specs=pl.BlockSpec((channels, leaf_count), lambda s: (0, 0)),
        scratch_shapes=[pltpu.VMEM((batch * channels, leaf_count), jnp.bfloat16)],
        compiler_params=pltpu.CompilerParams(vmem_limit_bytes=48 << 20),
        name="translate",
    )(lists, windows, direct_ops, image_ops)


def local(
    positions,
    charges,
    counts,
    owners,
    leaves,
    near_lists,
    image_lists,
    upward,
    child_ops,
    direct_ops,
    image_ops,
):
    box_count = lax.axis_size("box")
    depth_count = lax.axis_size("depth")
    devices = box_count * depth_count
    blocks = positions.shape[1]
    capacity = 2 * blocks // devices
    leaf_count = near_lists.shape[2]
    channels = upward.shape[0]
    sent = routed_sources(positions, charges, counts, owners, leaves, devices, capacity)
    windows, multipole = exchange(sent, upward, leaf_count)
    children = (
        multipole.reshape(channels, leaf_count // 8, 8)
        .transpose(0, 2, 1)
        .reshape(channels * 8, leaf_count // 8)
    )
    parents = jnp.dot(child_ops, children, preferred_element_type=jnp.float32)

    lists = jnp.concatenate([near_lists[:, 0, :], image_lists[:, 0, :]], axis=0)
    potentials = translate(lists, windows, direct_ops.T, image_ops.T)
    return (potentials[:, None, :], parents[:, None, :])


def solution(mesh):
    return jax.shard_map(
        local,
        mesh=mesh,
        in_specs=(
            P(None, ("box", "depth"), None),
            P(None, ("box", "depth"), None),
            P(("box", "depth")),
            P(("box", "depth"), None),
            P(("box", "depth")),
            P(None, "depth", "box"),
            P(None, "depth", "box"),
            P(),
            P(),
            P(),
            P(),
        ),
        out_specs=(P(None, "depth", "box"), P(None, "depth", "box")),
        check_vma=False,
    )
```

```python
import functools

import jax
import jax.numpy as jnp
import numpy as np
from jax import lax
from jax.experimental import pallas as pl
from jax.experimental.pallas import tpu as pltpu
from jax.sharding import PartitionSpec as P
from numpy.polynomial import chebyshev, polynomial

GRID = 6
LANES = 384
VM = pl.BlockSpec(memory_space=pltpu.VMEM)
HBM = pl.BlockSpec(memory_space=pltpu.HBM)
SM = pl.BlockSpec(memory_space=pltpu.SMEM)


def surface_index(grid_size):
    indices = np.arange(grid_size)
    lattice = np.stack(np.meshgrid(indices, indices, indices, indexing="ij"), -1).reshape(-1, 3)
    outside = np.any((lattice == 0) | (lattice == grid_size - 1), axis=1)
    return lattice[outside].astype(np.int32)


def node_coordinates(grid_size):
    middle = (grid_size - 1) / 2.0
    return ((np.arange(grid_size) - middle) * (1.5 / middle)).astype(np.float32)


def series(function, degree):
    fitted = chebyshev.Chebyshev.interpolate(function, degree, domain=[1.0, 12.0])
    return [float(value) for value in fitted.convert(kind=polynomial.Polynomial).coef]


HALF_SINE = series(lambda s: np.sin(np.sqrt(s) / 2) / (np.sqrt(s) / 2), 4)
HALF_COSINE = series(lambda s: np.cos(np.sqrt(s) / 2), 5)


def horner(coefficients, s):
    value = coefficients[-1] * s + coefficients[-2]
    for coefficient in coefficients[-3::-1]:
        value = value * s + coefficient
    return value


def waves(s):
    sine = horner(HALF_SINE, s)
    cosine = horner(HALF_COSINE, s)
    sine = sine * cosine
    cosine = cosine * cosine
    cosine = (cosine + cosine) - 1.0
    twice = cosine + cosine
    return (twice * cosine - 1.0) * lax.rsqrt(s), twice * sine


def pieces(value, count=3):
    terms = []
    for _ in range(count):
        terms.append(value.astype(jnp.bfloat16))
        value = value - terms[-1].astype(jnp.float32)
    return terms


def source_sums(table, positions, charges, counts, planes, depths, live_charges, values):
    nodes = node_coordinates(GRID)
    blocks, rows = positions.shape[1:]
    x, y, z = positions[0].T, positions[1].T, positions[2].T
    squares = []
    for node in nodes:
        delta = float(node) - y
        squares.append(delta * delta)
    for i, node in enumerate(nodes):
        delta = float(node) - x
        delta = delta * delta
        for j in range(len(nodes)):
            planes[i * len(nodes) + j] = delta + squares[j]
        delta = float(node) - z
        depths[i] = delta * delta
    live = lax.broadcasted_iota(jnp.int32, (rows, blocks), 0) < counts[...]
    for part in range(2):
        live_charges[part] = jnp.where(live, charges[part].T, 0.0)
    points = table.shape[1]

    def one_point(p, carry):
        plane = table[0, p]
        depth = table[1, p]
        real = imaginary = None
        for chunk in range(rows // 8):
            place = pl.ds(8 * chunk, 8)
            cosine, sine = waves(planes[plane, place, :] + depths[depth, place, :])
            first = live_charges[0, place, :]
            second = live_charges[1, place, :]
            a = cosine * first - sine * second
            b = sine * first + cosine * second
            real = a if real is None else real + a
            imaginary = b if imaginary is None else imaginary + b
        values[pl.ds(p, 1), :] = jnp.sum(real, axis=0, keepdims=True)
        values[pl.ds(points + p, 1), :] = jnp.sum(imaginary, axis=0, keepdims=True)
        return carry

    lax.fori_loop(0, points, one_point, 0)


def fill_slots(values, owners, sent):
    devices, capacity, _ = sent.shape
    blocks = owners.shape[1]
    shape = (blocks, blocks)
    target = jnp.broadcast_to(owners[...].astype(jnp.float32), shape)
    earlier = (target == target.T) & (
        lax.broadcasted_iota(jnp.int32, shape, 0) < lax.broadcasted_iota(jnp.int32, shape, 1)
    )
    rank = jnp.sum(jnp.where(earlier, 1.0, 0.0), axis=0, keepdims=True)
    terms = pieces(values[...])
    device = lax.broadcasted_iota(jnp.int32, (devices, blocks), 0)
    for place in range(capacity):
        pick = jnp.where((device == owners[...]) & (rank == place), 1.0, 0.0).astype(jnp.bfloat16)
        sent[:, place, :] = sum(
            lax.dot_general(pick, term, (((1,), (1,)), ((), ())), preferred_element_type=jnp.float32)
            for term in terms
        )


def raise_arrived(arrived, upward, leaf_count):
    devices, capacity, _ = arrived.shape
    channels = upward.shape[0]
    values = jnp.concatenate([arrived[:, place, :] for place in range(capacity)], axis=0)
    leaf = values[:, channels : channels + 1].astype(jnp.int32)
    members = jnp.where(
        lax.broadcasted_iota(jnp.int32, (devices * capacity, leaf_count), 1) == leaf, 1.0, 0.0
    ).astype(jnp.bfloat16)
    raised = lax.dot_general(
        upward[...],
        values[:, :channels],
        (((1,), (1,)), ((), ())),
        precision=lax.Precision.HIGHEST,
        preferred_element_type=jnp.float32,
    )
    summed = sum(
        jnp.dot(term, members, preferred_element_type=jnp.float32) for term in pieces(raised)
    )
    return summed.astype(jnp.bfloat16)


def parents_of(multipole, child_ops):
    channels, leaf_count = multipole.shape
    family = child_ops.shape[1] // channels
    wide = jnp.broadcast_to(
        multipole.astype(jnp.float32)[:, None, :], (channels, family, leaf_count)
    )
    shape = (channels, family, leaf_count)
    mine = lax.broadcasted_iota(jnp.int32, shape, 2) % family == lax.broadcasted_iota(
        jnp.int32, shape, 1
    )
    children = jnp.where(mine, wide, 0.0).reshape(channels * family, leaf_count)
    spread = jnp.dot(
        child_ops[...], children.astype(jnp.bfloat16), preferred_element_type=jnp.float32
    )
    shape = (leaf_count // family, leaf_count)
    group = jnp.where(
        lax.broadcasted_iota(jnp.int32, shape, 1) // family
        == lax.broadcasted_iota(jnp.int32, shape, 0),
        1.0,
        0.0,
    ).astype(jnp.bfloat16)
    return sum(
        lax.dot_general(group, term, (((1,), (1,)), ((), ())), preferred_element_type=jnp.float32)
        for term in pieces(spread)
    )


def step_kernel(
    table,
    positions_in,
    charges_in,
    counts_in,
    owners_in,
    leaves_in,
    near_in,
    image_in,
    upward_in,
    child_in,
    direct_in,
    mirrored_in,
    potentials,
    parents,
    positions,
    charges,
    counts,
    owners,
    leaves,
    lists,
    upward,
    child_ops,
    operators,
    planes,
    depths,
    live_charges,
    values,
    sent,
    arrived,
    windows,
    gathered,
    input_sem,
    operator_sem,
    send_sem,
    arrive_sem,
    halo_send,
    halo_recv,
):
    box, depth = lax.axis_index("box"), lax.axis_index("depth")
    boxes, slabs = lax.axis_size("box"), lax.axis_size("depth")
    devices, capacity, _ = sent.shape
    channels, leaf_count = potentials.shape
    offsets = near_in.shape[0]
    steps, _, width = operators.shape
    batch = width // channels
    half = steps // 2
    me = box * slabs + depth

    fetches = [
        pltpu.make_async_copy(source, place, input_sem.at[number])
        for number, (source, place) in enumerate(
            [
                (positions_in, positions),
                (charges_in, charges),
                (counts_in, counts),
                (owners_in, owners),
                (leaves_in, leaves),
                (near_in, lists.at[pl.ds(0, offsets)]),
                (image_in, lists.at[pl.ds(offsets, offsets)]),
                (upward_in, upward),
                (child_in, child_ops),
            ]
        )
    ]
    for fetch in fetches:
        fetch.start()
    for step in range(steps):
        pltpu.make_async_copy(
            (direct_in if step < half else mirrored_in).at[
                :, pl.ds(step % half * width, width)
            ],
            operators.at[step],
            operator_sem.at[step],
        ).start()

    def coordinates(device):
        return (device // slabs, lax.rem(device, slabs))

    barrier = pltpu.get_barrier_semaphore()

    def greet(j, carry):
        pl.semaphore_signal(
            barrier,
            inc=1,
            device_id=coordinates(lax.rem(me + j, devices)),
            device_id_type=pl.DeviceIdType.MESH,
        )
        return carry

    lax.fori_loop(1, devices, greet, 0)
    values[...] = jnp.zeros_like(values)
    for fetch in fetches:
        fetch.wait()
    source_sums(table, positions, charges, counts, planes, depths, live_charges, values)
    values[pl.ds(channels, 1), :] = leaves[...].astype(jnp.float32)
    fill_slots(values, owners, sent)
    pl.semaphore_wait(barrier, devices - 1)

    def route(j, carry):
        target = lax.rem(me + j, devices)
        pltpu.make_async_remote_copy(
            src_ref=sent.at[target],
            dst_ref=arrived.at[me],
            send_sem=send_sem,
            recv_sem=arrive_sem,
            device_id=coordinates(target),
            device_id_type=pl.DeviceIdType.MESH,
        ).start()
        return carry

    lax.fori_loop(1, devices, route, 0)
    arrived[me] = sent[me]
    others = pl.ds(0, devices - 1)
    every = pltpu.make_async_remote_copy(
        src_ref=sent.at[others],
        dst_ref=arrived.at[others],
        send_sem=send_sem,
        recv_sem=arrive_sem,
        device_id=(lax.rem(box + 1, boxes), depth),
        device_id_type=pl.DeviceIdType.MESH,
    )
    every.wait_send()
    every.wait_recv()
    windows[0, 1] = raise_arrived(arrived, upward, leaf_count)

    def copy(number, source, place, device):
        return pltpu.make_async_remote_copy(
            src_ref=windows.at[source],
            dst_ref=windows.at[place],
            send_sem=halo_send.at[number],
            recv_sem=halo_recv.at[number],
            device_id=device,
            device_id_type=pl.DeviceIdType.MESH,
        )

    def beside(number, slab):
        to_right = copy(number, (slab, 1), (slab, 0), (box + 1, depth))
        to_left = copy(number + 1, (slab, 1), (slab, 2), (box - 1, depth))
        return to_right, to_left

    mirror = copy(4, (0, 1), (1, 1), (box, slabs - 1 - depth))
    direct, image = beside(0, 0), beside(2, 1)
    has_left, has_right = box > 0, box < boxes - 1
    blank = jnp.zeros((channels, leaf_count), jnp.bfloat16)

    def start(pair):
        @pl.when(has_right)
        def _():
            pair[0].start()

        @pl.when(has_left)
        def _():
            pair[1].start()

    def receive(pair):
        @pl.when(has_left)
        def _():
            pair[0].wait_recv()

        @pl.when(has_right)
        def _():
            pair[1].wait_recv()

    def sent_off(pair):
        @pl.when(has_right)
        def _():
            pair[0].wait_send()

        @pl.when(has_left)
        def _():
            pair[1].wait_send()

    start(direct)
    mirror.start()

    @pl.when(jnp.logical_not(has_left))
    def _():
        windows[0, 0] = blank
        windows[1, 0] = blank

    @pl.when(jnp.logical_not(has_right))
    def _():
        windows[0, 2] = blank
        windows[1, 2] = blank

    parents[...] = parents_of(windows[0, 1], child_ops)
    potentials[...] = jnp.zeros_like(potentials)
    receive(direct)
    row = lax.broadcasted_iota(jnp.int32, (leaf_count, leaf_count), 0)

    def translate(step, carry):
        @pl.when(step == half // 2)
        def _():
            mirror.wait_recv()
            start(image)

        @pl.when(step == half)
        def _():
            receive(image)

        pltpu.make_async_copy(
            direct_in.at[:, pl.ds(0, width)], operators.at[step], operator_sem.at[step]
        ).wait()
        slab = step // half
        window = jnp.concatenate([windows[slab, part] for part in range(3)], axis=1)
        for o in range(batch):
            chosen = lists[step * batch + o]
            hot = jnp.concatenate(
                [
                    jnp.where(row == chosen - part * leaf_count, 1.0, 0.0).astype(jnp.bfloat16)
                    for part in range(3)
                ],
                axis=0,
            )
            picked = jnp.dot(window, hot, preferred_element_type=jnp.float32)
            gathered[pl.ds(o * channels, channels), :] = picked.astype(jnp.bfloat16)
        potentials[...] += jnp.dot(
            operators[step], gathered[...], preferred_element_type=jnp.float32
        )
        return carry

    lax.fori_loop(0, steps, translate, 0)
    sent_off(direct)
    sent_off(image)
    mirror.wait_send()


def local(
    positions,
    charges,
    counts,
    owners,
    leaves,
    near_lists,
    image_lists,
    upward,
    child_ops,
    direct_ops,
    image_ops,
):
    devices = lax.axis_size("box") * lax.axis_size("depth")
    blocks, rows = positions.shape[1:]
    capacity = 2 * blocks // devices
    offsets, _, leaf_count = near_lists.shape
    channels = upward.shape[0]
    index = surface_index(GRID)
    table = jnp.asarray(np.stack([index[:, 0] * GRID + index[:, 1], index[:, 2]]))
    batch = 16
    steps = 2 * offsets // batch
    parent_count = leaf_count * channels // child_ops.shape[1]

    def scratch(*shape, dtype=jnp.float32):
        return pltpu.VMEM(shape, dtype)

    potentials, parents = pl.pallas_call(
        step_kernel,
        out_shape=(
            jax.ShapeDtypeStruct((channels, leaf_count), jnp.float32),
            jax.ShapeDtypeStruct((parent_count, channels), jnp.float32),
        ),
        in_specs=[SM] + [HBM] * 11,
        out_specs=(VM, VM),
        scratch_shapes=[
            scratch(*positions.shape),
            scratch(*charges.shape),
            scratch(1, blocks, dtype=jnp.int32),
            scratch(1, blocks, dtype=jnp.int32),
            scratch(1, blocks, dtype=jnp.int32),
            scratch(2 * offsets, 1, leaf_count, dtype=jnp.int32),
            scratch(*upward.shape),
            scratch(*child_ops.shape, dtype=jnp.bfloat16),
            scratch(steps, channels, batch * channels, dtype=jnp.bfloat16),
            scratch(GRID * GRID, rows, blocks),
            scratch(GRID, rows, blocks),
            scratch(2, rows, blocks),
            scratch(LANES, blocks),
            scratch(devices, capacity, LANES),
            scratch(devices, capacity, LANES),
            scratch(2, 3, channels, leaf_count, dtype=jnp.bfloat16),
            scratch(batch * channels, leaf_count, dtype=jnp.bfloat16),
            pltpu.SemaphoreType.DMA((9,)),
            pltpu.SemaphoreType.DMA((steps,)),
            pltpu.SemaphoreType.DMA,
            pltpu.SemaphoreType.DMA,
            pltpu.SemaphoreType.DMA((5,)),
            pltpu.SemaphoreType.DMA((5,)),
        ],
        compiler_params=pltpu.CompilerParams(
            vmem_limit_bytes=56 << 20, has_side_effects=True, collective_id=0
        ),
        name="step",
    )(
        table,
        positions,
        charges,
        counts.reshape(1, blocks),
        owners.reshape(1, blocks),
        leaves.reshape(1, blocks),
        near_lists,
        image_lists,
        upward,
        child_ops,
        direct_ops.T,
        image_ops.T,
    )
    return (potentials[:, None, :], parents.T[:, None, :])


def solution(mesh):
    return jax.shard_map(
        local,
        mesh=mesh,
        in_specs=(
            P(None, ("box", "depth"), None),
            P(None, ("box", "depth"), None),
            P(("box", "depth")),
            P(("box", "depth"), None),
            P(("box", "depth")),
            P(None, "depth", "box"),
            P(None, "depth", "box"),
            P(),
            P(),
            P(),
            P(),
        ),
        out_specs=(P(None, "depth", "box"), P(None, "depth", "box")),
        check_vma=False,
    )
```

```python
import functools

import jax
import jax.numpy as jnp
import numpy as np
from jax import lax
from jax.experimental import pallas as pl
from jax.experimental.pallas import tpu as pltpu
from jax.sharding import PartitionSpec as P
from numpy.polynomial import chebyshev, polynomial

GRID = 6
VM = pl.BlockSpec(memory_space=pltpu.VMEM)
HBM = pl.BlockSpec(memory_space=pltpu.HBM)
SM = pl.BlockSpec(memory_space=pltpu.SMEM)


def surface_index(grid_size):
    indices = np.arange(grid_size)
    lattice = np.stack(np.meshgrid(indices, indices, indices, indexing="ij"), -1).reshape(-1, 3)
    outside = np.any((lattice == 0) | (lattice == grid_size - 1), axis=1)
    return lattice[outside].astype(np.int32)


def node_coordinates(grid_size):
    middle = (grid_size - 1) / 2.0
    return ((np.arange(grid_size) - middle) * (1.5 / middle)).astype(np.float32)


def series(function, degree):
    fitted = chebyshev.Chebyshev.interpolate(function, degree, domain=[1.0, 12.0])
    return [float(value) for value in fitted.convert(kind=polynomial.Polynomial).coef]


HALF_SINE = series(lambda s: np.sin(np.sqrt(s) / 2) / (np.sqrt(s) / 2), 4)
HALF_COSINE = series(lambda s: np.cos(np.sqrt(s) / 2), 5)


SCALE = 2.0 * HALF_SINE[-1] * HALF_COSINE[-1]


def monic(coefficients, s):
    value = s + coefficients[-2] / coefficients[-1]
    for coefficient in coefficients[-3::-1]:
        value = value * s + coefficient / coefficients[-1]
    return value


def waves(s):
    sine = monic(HALF_SINE, s)
    cosine = monic(HALF_COSINE, s)
    sine = sine * cosine
    cosine = cosine * cosine * (2.0 * HALF_COSINE[-1] ** 2) - 1.0
    return (cosine * cosine - 0.5) * lax.rsqrt(s), sine * cosine


def pieces(value, count=3):
    terms = []
    for _ in range(count):
        terms.append(value.astype(jnp.bfloat16))
        value = value - terms[-1].astype(jnp.float32)
    return terms


def source_sums(table, positions, charges, counts, planes, depths, live_charges, values):
    nodes = node_coordinates(GRID)
    blocks, rows = positions.shape[1:]
    x, y, z = positions[0].T, positions[1].T, positions[2].T
    squares = []
    for node in nodes:
        delta = float(node) - y
        squares.append(delta * delta)
    for i, node in enumerate(nodes):
        delta = float(node) - x
        delta = delta * delta
        for j in range(len(nodes)):
            planes[i * len(nodes) + j] = delta + squares[j]
        delta = float(node) - z
        depths[i] = delta * delta
    live = lax.broadcasted_iota(jnp.int32, (rows, blocks), 0) < counts[...]
    for part in range(2):
        charge = jnp.where(live, charges[part].T, 0.0)
        live_charges[part] = 2.0 * charge
        live_charges[2 + part] = SCALE * charge
    points = table.shape[1]

    def one_point(p, carry):
        plane = table[0, p]
        depth = table[1, p]
        real = imaginary = None
        for chunk in range(rows // 8):
            place = pl.ds(8 * chunk, 8)
            cosine, sine = waves(planes[plane, place, :] + depths[depth, place, :])
            a = cosine * live_charges[0, place, :] - sine * live_charges[3, place, :]
            b = sine * live_charges[2, place, :] + cosine * live_charges[1, place, :]
            real = a if real is None else real + a
            imaginary = b if imaginary is None else imaginary + b
        values[pl.ds(p, 1), :] = jnp.sum(real, axis=0, keepdims=True)
        values[pl.ds(points + p, 1), :] = jnp.sum(imaginary, axis=0, keepdims=True)
        return carry

    lax.fori_loop(0, points, one_point, 0, unroll=4)


def fill_slots(values, owners, leaves, sent, capacity):
    devices, _, width = sent.shape
    channels, blocks = values.shape
    shape = (blocks, blocks)
    target = jnp.broadcast_to(owners[...].astype(jnp.float32), shape)
    earlier = (target == target.T) & (
        lax.broadcasted_iota(jnp.int32, shape, 0) < lax.broadcasted_iota(jnp.int32, shape, 1)
    )
    rank = jnp.sum(jnp.where(earlier, 1.0, 0.0), axis=0, keepdims=True)
    device = lax.broadcasted_iota(jnp.int32, (devices, blocks), 0)
    spare = width - capacity * channels
    place_row = lax.broadcasted_iota(jnp.int32, (spare, blocks), 0)
    leaf = jnp.broadcast_to(leaves[...].astype(jnp.float32), (spare, blocks))
    filled = None
    for place in range(capacity):
        pick = jnp.where((device == owners[...]) & (rank == place), 1.0, 0.0).astype(jnp.bfloat16)
        column = jnp.concatenate(
            [
                values[...] if other == place else jnp.zeros((channels, blocks), jnp.float32)
                for other in range(capacity)
            ]
            + [jnp.where(place_row == place, leaf, 0.0)],
            axis=0,
        )
        for term in pieces(column):
            part = lax.dot_general(
                pick, term, (((1,), (1,)), ((), ())), preferred_element_type=jnp.float32
            )
            filled = part if filled is None else filled + part
    sent[:, 0, :] = filled


def raise_arrived(arrived, upward, leaf_count, capacity):
    devices = arrived.shape[0]
    channels = upward.shape[0]
    rows = arrived[:, 0, :]
    first = capacity * channels
    values = jnp.concatenate(
        [rows[:, place * channels : (place + 1) * channels] for place in range(capacity)], axis=0
    )
    leaf = jnp.concatenate(
        [rows[:, first + place : first + place + 1] for place in range(capacity)], axis=0
    ).astype(jnp.int32)
    members = jnp.where(
        lax.broadcasted_iota(jnp.int32, (devices * capacity, leaf_count), 1) == leaf, 1.0, 0.0
    ).astype(jnp.bfloat16)
    raised = lax.dot_general(
        upward[...],
        values,
        (((1,), (1,)), ((), ())),
        precision=lax.Precision.HIGHEST,
        preferred_element_type=jnp.float32,
    )
    summed = sum(
        jnp.dot(term, members, preferred_element_type=jnp.float32) for term in pieces(raised)
    )
    return summed.astype(jnp.bfloat16)


def parents_of(multipole, child_ops):
    channels, leaf_count = multipole.shape
    family = child_ops.shape[1] // channels
    wide = jnp.broadcast_to(
        multipole.astype(jnp.float32)[:, None, :], (channels, family, leaf_count)
    )
    shape = (channels, family, leaf_count)
    mine = lax.broadcasted_iota(jnp.int32, shape, 2) % family == lax.broadcasted_iota(
        jnp.int32, shape, 1
    )
    children = jnp.where(mine, wide, 0.0).reshape(channels * family, leaf_count)
    spread = jnp.dot(
        child_ops[...], children.astype(jnp.bfloat16), preferred_element_type=jnp.float32
    )
    shape = (leaf_count // family, leaf_count)
    group = jnp.where(
        lax.broadcasted_iota(jnp.int32, shape, 1) // family
        == lax.broadcasted_iota(jnp.int32, shape, 0),
        1.0,
        0.0,
    ).astype(jnp.bfloat16)
    return sum(
        lax.dot_general(group, term, (((1,), (1,)), ((), ())), preferred_element_type=jnp.float32)
        for term in pieces(spread)
    )


def step_kernel(
    table,
    positions_in,
    charges_in,
    counts_in,
    owners_in,
    leaves_in,
    near_in,
    image_in,
    upward_in,
    child_in,
    direct_in,
    mirrored_in,
    potentials,
    parents,
    positions,
    charges,
    counts,
    owners,
    leaves,
    lists,
    upward,
    child_ops,
    operators,
    planes,
    depths,
    live_charges,
    values,
    sent,
    arrived,
    windows,
    gathered,
    input_sem,
    operator_sem,
    send_sem,
    arrive_sem,
    halo_send,
    halo_recv,
):
    box, depth = lax.axis_index("box"), lax.axis_index("depth")
    boxes, slabs = lax.axis_size("box"), lax.axis_size("depth")
    devices = sent.shape[0]
    channels, leaf_count = potentials.shape
    capacity = sent.shape[2] // channels
    offsets = near_in.shape[0]
    steps, _, width = operators.shape
    batch = width // channels
    half = steps // 2
    me = box * slabs + depth

    fetches = [
        pltpu.make_async_copy(source, place, input_sem.at[number])
        for number, (source, place) in enumerate(
            [
                (positions_in, positions),
                (charges_in, charges),
                (counts_in, counts),
                (owners_in, owners),
                (leaves_in, leaves),
                (near_in, lists.at[pl.ds(0, offsets)]),
                (image_in, lists.at[pl.ds(offsets, offsets)]),
                (upward_in, upward),
                (child_in, child_ops),
            ]
        )
    ]
    for fetch in fetches[:5]:
        fetch.start()
    barrier = pltpu.get_barrier_semaphore()
    columns = [lax.rem(depth + ahead, slabs) for ahead in range(slabs)]

    def every_device(send):
        def one_row(ahead, carry):
            target_box = lax.rem(box + ahead, boxes)
            for column in columns:
                send(target_box, column)
            return carry

        for column in columns[1:]:
            send(box, column)
        lax.fori_loop(1, boxes, one_row, 0)

    def greet(target_box, target_depth):
        pl.semaphore_signal(
            barrier,
            inc=1,
            device_id=(target_box, target_depth),
            device_id_type=pl.DeviceIdType.MESH,
        )

    every_device(greet)
    for fetch in fetches[:5]:
        fetch.wait()
    for fetch in fetches[5:]:
        fetch.start()
    for step in range(steps):
        pltpu.make_async_copy(
            (direct_in if step < half else mirrored_in).at[
                :, pl.ds(step % half * width, width)
            ],
            operators.at[step],
            operator_sem.at[step],
        ).start()
    source_sums(table, positions, charges, counts, planes, depths, live_charges, values)
    fill_slots(values, owners, leaves, sent, capacity)
    pl.semaphore_wait(barrier, devices - 1)

    def route(target_box, target_depth):
        pltpu.make_async_remote_copy(
            src_ref=sent.at[target_box * slabs + target_depth],
            dst_ref=arrived.at[me],
            send_sem=send_sem,
            recv_sem=arrive_sem,
            device_id=(target_box, target_depth),
            device_id_type=pl.DeviceIdType.MESH,
        ).start()

    every_device(route)
    arrived[me] = sent[me]
    others = pl.ds(0, devices - 1)
    every = pltpu.make_async_remote_copy(
        src_ref=sent.at[others],
        dst_ref=arrived.at[others],
        send_sem=send_sem,
        recv_sem=arrive_sem,
        device_id=(lax.rem(box + 1, boxes), depth),
        device_id_type=pl.DeviceIdType.MESH,
    )
    for fetch in fetches[5:]:
        fetch.wait()
    every.wait_send()
    every.wait_recv()
    windows[0, 1] = raise_arrived(arrived, upward, leaf_count, capacity)

    def copy(number, source, place, device):
        return pltpu.make_async_remote_copy(
            src_ref=windows.at[source],
            dst_ref=windows.at[place],
            send_sem=halo_send.at[number],
            recv_sem=halo_recv.at[number],
            device_id=device,
            device_id_type=pl.DeviceIdType.MESH,
        )

    def beside(number, slab):
        to_right = copy(number, (slab, 1), (slab, 0), (box + 1, depth))
        to_left = copy(number + 1, (slab, 1), (slab, 2), (box - 1, depth))
        return to_right, to_left

    mirror = copy(4, (0, 1), (1, 1), (box, slabs - 1 - depth))
    direct, image = beside(0, 0), beside(2, 1)
    has_left, has_right = box > 0, box < boxes - 1
    blank = jnp.zeros((channels, leaf_count), jnp.bfloat16)

    def start(pair):
        @pl.when(has_right)
        def _():
            pair[0].start()

        @pl.when(has_left)
        def _():
            pair[1].start()

    def receive(pair):
        @pl.when(has_left)
        def _():
            pair[0].wait_recv()

        @pl.when(has_right)
        def _():
            pair[1].wait_recv()

    def sent_off(pair):
        @pl.when(has_right)
        def _():
            pair[0].wait_send()

        @pl.when(has_left)
        def _():
            pair[1].wait_send()

    start(direct)
    mirror.start()

    @pl.when(jnp.logical_not(has_left))
    def _():
        windows[0, 0] = blank
        windows[1, 0] = blank

    @pl.when(jnp.logical_not(has_right))
    def _():
        windows[0, 2] = blank
        windows[1, 2] = blank

    parents[...] = parents_of(windows[0, 1], child_ops)
    potentials[...] = jnp.zeros_like(potentials)
    receive(direct)
    row = lax.broadcasted_iota(jnp.int32, (leaf_count, leaf_count), 0)

    def translate(step, carry):
        @pl.when(step == half // 2)
        def _():
            mirror.wait_recv()
            start(image)

        @pl.when(step == half)
        def _():
            receive(image)

        pltpu.make_async_copy(
            direct_in.at[:, pl.ds(0, width)], operators.at[step], operator_sem.at[step]
        ).wait()
        slab = step // half
        window = jnp.concatenate([windows[slab, part] for part in range(3)], axis=1)
        for o in range(batch):
            chosen = lists[step * batch + o]
            hot = jnp.concatenate(
                [
                    jnp.where(row == chosen - part * leaf_count, 1.0, 0.0).astype(jnp.bfloat16)
                    for part in range(3)
                ],
                axis=0,
            )
            picked = jnp.dot(window, hot, preferred_element_type=jnp.float32)
            gathered[pl.ds(o * channels, channels), :] = picked.astype(jnp.bfloat16)
        potentials[...] += jnp.dot(
            operators[step], gathered[...], preferred_element_type=jnp.float32
        )
        return carry

    lax.fori_loop(0, steps, translate, 0)
    sent_off(direct)
    sent_off(image)
    mirror.wait_send()


def local(
    positions,
    charges,
    counts,
    owners,
    leaves,
    near_lists,
    image_lists,
    upward,
    child_ops,
    direct_ops,
    image_ops,
):
    devices = lax.axis_size("box") * lax.axis_size("depth")
    blocks, rows = positions.shape[1:]
    capacity = 2 * blocks // devices
    offsets, _, leaf_count = near_lists.shape
    channels = upward.shape[0]
    index = surface_index(GRID)
    table = jnp.asarray(np.stack([index[:, 0] * GRID + index[:, 1], index[:, 2]]))
    batch = 16
    steps = 2 * offsets // batch
    width = -(-capacity * (channels + 1) // 128) * 128
    parent_count = leaf_count * channels // child_ops.shape[1]

    def scratch(*shape, dtype=jnp.float32):
        return pltpu.VMEM(shape, dtype)

    potentials, parents = pl.pallas_call(
        step_kernel,
        out_shape=(
            jax.ShapeDtypeStruct((channels, leaf_count), jnp.float32),
            jax.ShapeDtypeStruct((parent_count, channels), jnp.float32),
        ),
        in_specs=[SM] + [HBM] * 11,
        out_specs=(VM, VM),
        scratch_shapes=[
            scratch(*positions.shape),
            scratch(*charges.shape),
            scratch(1, blocks, dtype=jnp.int32),
            scratch(1, blocks, dtype=jnp.int32),
            scratch(1, blocks, dtype=jnp.int32),
            scratch(2 * offsets, 1, leaf_count, dtype=jnp.int32),
            scratch(*upward.shape),
            scratch(*child_ops.shape, dtype=jnp.bfloat16),
            scratch(steps, channels, batch * channels, dtype=jnp.bfloat16),
            scratch(GRID * GRID, rows, blocks),
            scratch(GRID, rows, blocks),
            scratch(4, rows, blocks),
            scratch(channels, blocks),
            scratch(devices, 1, width),
            scratch(devices, 1, width),
            scratch(2, 3, channels, leaf_count, dtype=jnp.bfloat16),
            scratch(batch * channels, leaf_count, dtype=jnp.bfloat16),
            pltpu.SemaphoreType.DMA((9,)),
            pltpu.SemaphoreType.DMA((steps,)),
            pltpu.SemaphoreType.DMA,
            pltpu.SemaphoreType.DMA,
            pltpu.SemaphoreType.DMA((5,)),
            pltpu.SemaphoreType.DMA((5,)),
        ],
        compiler_params=pltpu.CompilerParams(
            vmem_limit_bytes=56 << 20, has_side_effects=True, collective_id=0
        ),
        name="step",
    )(
        table,
        positions,
        charges,
        counts.reshape(1, blocks),
        owners.reshape(1, blocks),
        leaves.reshape(1, blocks),
        near_lists,
        image_lists,
        upward,
        child_ops,
        direct_ops.T,
        image_ops.T,
    )
    return (potentials[:, None, :], parents.T[:, None, :])


def solution(mesh):
    return jax.shard_map(
        local,
        mesh=mesh,
        in_specs=(
            P(None, ("box", "depth"), None),
            P(None, ("box", "depth"), None),
            P(("box", "depth")),
            P(("box", "depth"), None),
            P(("box", "depth")),
            P(None, "depth", "box"),
            P(None, "depth", "box"),
            P(),
            P(),
            P(),
            P(),
        ),
        out_specs=(P(None, "depth", "box"), P(None, "depth", "box")),
        check_vma=False,
    )
```

```python
import functools

import jax
import jax.numpy as jnp
import numpy as np
from jax import lax
from jax.experimental import pallas as pl
from jax.experimental.pallas import tpu as pltpu
from jax.sharding import PartitionSpec as P
from numpy.polynomial import chebyshev, polynomial

GRID = 6
VM = pl.BlockSpec(memory_space=pltpu.VMEM)
HBM = pl.BlockSpec(memory_space=pltpu.HBM)
SM = pl.BlockSpec(memory_space=pltpu.SMEM)


def surface_index(grid_size):
    indices = np.arange(grid_size)
    lattice = np.stack(np.meshgrid(indices, indices, indices, indexing="ij"), -1).reshape(-1, 3)
    outside = np.any((lattice == 0) | (lattice == grid_size - 1), axis=1)
    return lattice[outside].astype(np.int32)


def node_coordinates(grid_size):
    middle = (grid_size - 1) / 2.0
    return ((np.arange(grid_size) - middle) * (1.5 / middle)).astype(np.float32)


def series(function, degree):
    fitted = chebyshev.Chebyshev.interpolate(function, degree, domain=[1.0, 12.0])
    return [float(value) for value in fitted.convert(kind=polynomial.Polynomial).coef]


HALF_SINE = series(lambda s: np.sin(np.sqrt(s) / 2) / (np.sqrt(s) / 2), 4)
HALF_COSINE = series(lambda s: np.cos(np.sqrt(s) / 2), 5)


SCALE = 2.0 * HALF_SINE[-1] * HALF_COSINE[-1]


def monic(coefficients, s):
    value = s + coefficients[-2] / coefficients[-1]
    for coefficient in coefficients[-3::-1]:
        value = value * s + coefficient / coefficients[-1]
    return value


def waves(s):
    sine = monic(HALF_SINE, s)
    cosine = monic(HALF_COSINE, s)
    sine = sine * cosine
    cosine = cosine * cosine * (2.0 * HALF_COSINE[-1] ** 2) - 1.0
    return (cosine * cosine - 0.5) * lax.rsqrt(s), sine * cosine


def pieces(value, count=3):
    terms = []
    for _ in range(count):
        terms.append(value.astype(jnp.bfloat16))
        value = value - terms[-1].astype(jnp.float32)
    return terms


def prepare_sources(positions, charges, counts, planes, depths, live_charges):
    nodes = node_coordinates(GRID)
    blocks, rows = positions.shape[1:]
    x, y, z = positions[0].T, positions[1].T, positions[2].T
    squares = []
    for node in nodes:
        delta = float(node) - y
        squares.append(delta * delta)
    for i, node in enumerate(nodes):
        delta = float(node) - x
        delta = delta * delta
        for j in range(len(nodes)):
            planes[i * len(nodes) + j] = delta + squares[j]
        delta = float(node) - z
        depths[i] = delta * delta
    live = lax.broadcasted_iota(jnp.int32, (rows, blocks), 0) < counts[...]
    for part in range(2):
        charge = jnp.where(live, charges[part].T, 0.0)
        live_charges[part] = 2.0 * charge
        live_charges[2 + part] = SCALE * charge


def sum_point(table, planes, depths, live_charges, values, first, p):
    plane = table[0, first + p]
    depth = table[1, first + p]
    real = imaginary = None
    for chunk in range(planes.shape[1] // 8):
        place = pl.ds(8 * chunk, 8)
        cosine, sine = waves(planes[plane, place, :] + depths[depth, place, :])
        a = cosine * live_charges[0, place, :] - sine * live_charges[3, place, :]
        b = sine * live_charges[2, place, :] + cosine * live_charges[1, place, :]
        real = a if real is None else real + a
        imaginary = b if imaginary is None else imaginary + b
    values[pl.ds(p, 1), :] = jnp.sum(real, axis=0, keepdims=True)
    values[pl.ds(values.shape[0] // 2 + p, 1), :] = jnp.sum(imaginary, axis=0, keepdims=True)


def ranks(owners):
    blocks = owners.shape[1]
    shape = (blocks, blocks)
    target = jnp.broadcast_to(owners[...].astype(jnp.float32), shape)
    earlier = (target == target.T) & (
        lax.broadcasted_iota(jnp.int32, shape, 0) < lax.broadcasted_iota(jnp.int32, shape, 1)
    )
    return jnp.sum(jnp.where(earlier, 1.0, 0.0), axis=0, keepdims=True)


def fill_slots(values, owners, rank, leaves, sent, capacity):
    devices, _, width = sent.shape
    channels, blocks = values.shape
    device = lax.broadcasted_iota(jnp.int32, (devices, blocks), 0)
    spare = width - capacity * channels
    place_row = lax.broadcasted_iota(jnp.int32, (spare, blocks), 0)
    leaf = jnp.broadcast_to(leaves[...].astype(jnp.float32), (spare, blocks))
    filled = None
    for place in range(capacity):
        pick = jnp.where((device == owners[...]) & (rank == place), 1.0, 0.0).astype(jnp.bfloat16)
        column = jnp.concatenate(
            [
                values[...] if other == place else jnp.zeros((channels, blocks), jnp.float32)
                for other in range(capacity)
            ]
            + [jnp.where(place_row == place, leaf, 0.0)],
            axis=0,
        )
        for term in pieces(column):
            part = lax.dot_general(
                pick, term, (((1,), (1,)), ((), ())), preferred_element_type=jnp.float32
            )
            filled = part if filled is None else filled + part
    sent[:, 0, :] = filled


def raise_part(arrived, upward, capacity, first, count):
    rows = arrived[:, 0, :]
    channels = 2 * count
    values = jnp.concatenate(
        [rows[:, place * channels : (place + 1) * channels] for place in range(capacity)], axis=0
    )
    points = upward.shape[1] // 2
    columns = jnp.concatenate(
        [upward[:, first : first + count], upward[:, points + first : points + first + count]],
        axis=1,
    )
    return lax.dot_general(
        columns,
        values,
        (((1,), (1,)), ((), ())),
        precision=lax.Precision.HIGHEST,
        preferred_element_type=jnp.float32,
    )


def add_up(raised, arrived, capacity, count, leaf_count):
    rows = arrived[:, 0, :]
    first = capacity * 2 * count
    leaf = jnp.concatenate(
        [rows[:, first + place : first + place + 1] for place in range(capacity)], axis=0
    ).astype(jnp.int32)
    members = jnp.where(
        lax.broadcasted_iota(jnp.int32, (leaf.shape[0], leaf_count), 1) == leaf, 1.0, 0.0
    ).astype(jnp.bfloat16)
    summed = sum(
        jnp.dot(term, members, preferred_element_type=jnp.float32) for term in pieces(raised)
    )
    return summed.astype(jnp.bfloat16)


def parents_of(multipole, child_ops):
    channels, leaf_count = multipole.shape
    family = child_ops.shape[1] // channels
    wide = jnp.broadcast_to(
        multipole.astype(jnp.float32)[:, None, :], (channels, family, leaf_count)
    )
    shape = (channels, family, leaf_count)
    mine = lax.broadcasted_iota(jnp.int32, shape, 2) % family == lax.broadcasted_iota(
        jnp.int32, shape, 1
    )
    children = jnp.where(mine, wide, 0.0).reshape(channels * family, leaf_count)
    spread = jnp.dot(
        child_ops[...], children.astype(jnp.bfloat16), preferred_element_type=jnp.float32
    )
    shape = (leaf_count // family, leaf_count)
    group = jnp.where(
        lax.broadcasted_iota(jnp.int32, shape, 1) // family
        == lax.broadcasted_iota(jnp.int32, shape, 0),
        1.0,
        0.0,
    ).astype(jnp.bfloat16)
    return sum(
        lax.dot_general(group, term, (((1,), (1,)), ((), ())), preferred_element_type=jnp.float32)
        for term in pieces(spread)
    )


def step_kernel(
    table,
    positions_in,
    charges_in,
    counts_in,
    owners_in,
    leaves_in,
    near_in,
    image_in,
    upward_in,
    child_in,
    direct_in,
    mirrored_in,
    potentials,
    parents,
    positions,
    charges,
    counts,
    owners,
    leaves,
    lists,
    upward,
    child_ops,
    operators,
    planes,
    depths,
    live_charges,
    early_values,
    late_values,
    early_sent,
    late_sent,
    early_arrived,
    late_arrived,
    windows,
    gathered,
    input_sem,
    operator_sem,
    send_sem,
    arrive_sem,
    halo_send,
    halo_recv,
):
    box, depth = lax.axis_index("box"), lax.axis_index("depth")
    boxes, slabs = lax.axis_size("box"), lax.axis_size("depth")
    devices = early_sent.shape[0]
    early, late = early_values.shape[0] // 2, late_values.shape[0] // 2
    channels, leaf_count = potentials.shape
    capacity = early_sent.shape[2] // (2 * early)
    offsets = near_in.shape[0]
    steps, _, width = operators.shape
    batch = width // channels
    half = steps // 2
    me = box * slabs + depth

    fetches = [
        pltpu.make_async_copy(source, place, input_sem.at[number])
        for number, (source, place) in enumerate(
            [
                (positions_in, positions),
                (charges_in, charges),
                (counts_in, counts),
                (owners_in, owners),
                (leaves_in, leaves),
                (near_in, lists.at[pl.ds(0, offsets)]),
                (image_in, lists.at[pl.ds(offsets, offsets)]),
                (upward_in, upward),
                (child_in, child_ops),
            ]
        )
    ]
    for fetch in fetches[:5]:
        fetch.start()
    barrier = pltpu.get_barrier_semaphore()
    columns = [lax.rem(depth + ahead, slabs) for ahead in range(slabs)]

    def own_row(send):
        for column in columns[1:]:
            send(box, column)

    def one_row(ahead, send):
        target_box = lax.rem(box + ahead, boxes)
        for column in columns:
            send(target_box, column)

    def other_rows(send):
        def body(ahead, carry):
            one_row(ahead, send)
            return carry

        lax.fori_loop(1, boxes, body, 0)

    def greet(target_box, target_depth):
        pl.semaphore_signal(
            barrier,
            inc=1,
            device_id=(target_box, target_depth),
            device_id_type=pl.DeviceIdType.MESH,
        )

    own_row(greet)
    other_rows(greet)
    for fetch in fetches[:5]:
        fetch.wait()
    for fetch in fetches[5:]:
        fetch.start()
    for step in range(steps):
        pltpu.make_async_copy(
            (direct_in if step < half else mirrored_in).at[
                :, pl.ds(step % half * width, width)
            ],
            operators.at[step],
            operator_sem.at[step],
        ).start()
    prepare_sources(positions, charges, counts, planes, depths, live_charges)
    rank = ranks(owners)

    def early_point(p, carry):
        sum_point(table, planes, depths, live_charges, early_values, 0, p)
        return carry

    lax.fori_loop(0, early, early_point, 0, unroll=4)
    fill_slots(early_values, owners, rank, leaves, early_sent, capacity)
    pl.semaphore_wait(barrier, devices - 1)

    def route(number, sent, arrived):
        def send(target_box, target_depth):
            pltpu.make_async_remote_copy(
                src_ref=sent.at[target_box * slabs + target_depth],
                dst_ref=arrived.at[me],
                send_sem=send_sem.at[number],
                recv_sem=arrive_sem.at[number],
                device_id=(target_box, target_depth),
                device_id_type=pl.DeviceIdType.MESH,
            ).start()

        return send

    def all_routed(number, sent, arrived):
        others = pl.ds(0, devices - 1)
        return pltpu.make_async_remote_copy(
            src_ref=sent.at[others],
            dst_ref=arrived.at[others],
            send_sem=send_sem.at[number],
            recv_sem=arrive_sem.at[number],
            device_id=(lax.rem(box + 1, boxes), depth),
            device_id_type=pl.DeviceIdType.MESH,
        )

    early_send = route(0, early_sent, early_arrived)
    late_send = route(1, late_sent, late_arrived)
    early_all = all_routed(0, early_sent, early_arrived)
    late_all = all_routed(1, late_sent, late_arrived)
    own_row(early_send)

    def late_points(pair):
        for p in range(2):
            sum_point(table, planes, depths, live_charges, late_values, early, 2 * pair + p)

    def late_and_send(pair, carry):
        late_points(pair)
        one_row(pair + 1, early_send)
        return carry

    def late_only(pair, carry):
        late_points(pair)
        return carry

    lax.fori_loop(0, boxes - 1, late_and_send, 0)
    lax.fori_loop(boxes - 1, late // 2, late_only, 0)
    fill_slots(late_values, owners, rank, leaves, late_sent, capacity)
    own_row(late_send)
    other_rows(late_send)
    early_arrived[me] = early_sent[me]
    late_arrived[me] = late_sent[me]
    for fetch in fetches[5:]:
        fetch.wait()
    early_all.wait_recv()
    raised = raise_part(early_arrived, upward, capacity, 0, early)
    late_all.wait_recv()
    raised += raise_part(late_arrived, upward, capacity, early, late)
    windows[0, 1] = add_up(raised, late_arrived, capacity, late, leaf_count)

    def copy(number, source, place, device):
        return pltpu.make_async_remote_copy(
            src_ref=windows.at[source],
            dst_ref=windows.at[place],
            send_sem=halo_send.at[number],
            recv_sem=halo_recv.at[number],
            device_id=device,
            device_id_type=pl.DeviceIdType.MESH,
        )

    def beside(number, slab):
        to_right = copy(number, (slab, 1), (slab, 0), (box + 1, depth))
        to_left = copy(number + 1, (slab, 1), (slab, 2), (box - 1, depth))
        return to_right, to_left

    mirror = copy(4, (0, 1), (1, 1), (box, slabs - 1 - depth))
    direct, image = beside(0, 0), beside(2, 1)
    has_left, has_right = box > 0, box < boxes - 1
    blank = jnp.zeros((channels, leaf_count), jnp.bfloat16)

    def start(pair):
        @pl.when(has_right)
        def _():
            pair[0].start()

        @pl.when(has_left)
        def _():
            pair[1].start()

    def receive(pair):
        @pl.when(has_left)
        def _():
            pair[0].wait_recv()

        @pl.when(has_right)
        def _():
            pair[1].wait_recv()

    def sent_off(pair):
        @pl.when(has_right)
        def _():
            pair[0].wait_send()

        @pl.when(has_left)
        def _():
            pair[1].wait_send()

    start(direct)
    mirror.start()

    @pl.when(jnp.logical_not(has_left))
    def _():
        windows[0, 0] = blank
        windows[1, 0] = blank

    @pl.when(jnp.logical_not(has_right))
    def _():
        windows[0, 2] = blank
        windows[1, 2] = blank

    parents[...] = parents_of(windows[0, 1], child_ops)
    potentials[...] = jnp.zeros_like(potentials)
    receive(direct)
    row = lax.broadcasted_iota(jnp.int32, (leaf_count, leaf_count), 0)

    def translate(step, carry):
        @pl.when(step == half // 2)
        def _():
            mirror.wait_recv()
            start(image)

        @pl.when(step == half)
        def _():
            receive(image)

        pltpu.make_async_copy(
            direct_in.at[:, pl.ds(0, width)], operators.at[step], operator_sem.at[step]
        ).wait()
        slab = step // half
        window = jnp.concatenate([windows[slab, part] for part in range(3)], axis=1)
        for o in range(batch):
            chosen = lists[step * batch + o]
            hot = jnp.concatenate(
                [
                    jnp.where(row == chosen - part * leaf_count, 1.0, 0.0).astype(jnp.bfloat16)
                    for part in range(3)
                ],
                axis=0,
            )
            picked = jnp.dot(window, hot, preferred_element_type=jnp.float32)
            gathered[pl.ds(o * channels, channels), :] = picked.astype(jnp.bfloat16)
        potentials[...] += jnp.dot(
            operators[step], gathered[...], preferred_element_type=jnp.float32
        )
        return carry

    lax.fori_loop(0, steps, translate, 0)
    early_all.wait_send()
    late_all.wait_send()
    sent_off(direct)
    sent_off(image)
    mirror.wait_send()


def local(
    positions,
    charges,
    counts,
    owners,
    leaves,
    near_lists,
    image_lists,
    upward,
    child_ops,
    direct_ops,
    image_ops,
):
    devices = lax.axis_size("box") * lax.axis_size("depth")
    blocks, rows = positions.shape[1:]
    capacity = 2 * blocks // devices
    offsets, _, leaf_count = near_lists.shape
    channels = upward.shape[0]
    index = surface_index(GRID)
    table = jnp.asarray(np.stack([index[:, 0] * GRID + index[:, 1], index[:, 2]]))
    batch = 32
    steps = 2 * offsets // batch
    points = channels // 2
    early = points * 11 // 16 // 8 * 8
    parts = (early, points - early)
    widths = [-(-capacity * (2 * part + 1) // 128) * 128 for part in parts]
    parent_count = leaf_count * channels // child_ops.shape[1]

    def scratch(*shape, dtype=jnp.float32):
        return pltpu.VMEM(shape, dtype)

    potentials, parents = pl.pallas_call(
        step_kernel,
        out_shape=(
            jax.ShapeDtypeStruct((channels, leaf_count), jnp.float32),
            jax.ShapeDtypeStruct((parent_count, channels), jnp.float32),
        ),
        in_specs=[SM] + [HBM] * 11,
        out_specs=(VM, VM),
        scratch_shapes=[
            scratch(*positions.shape),
            scratch(*charges.shape),
            scratch(1, blocks, dtype=jnp.int32),
            scratch(1, blocks, dtype=jnp.int32),
            scratch(1, blocks, dtype=jnp.int32),
            scratch(2 * offsets, 1, leaf_count, dtype=jnp.int32),
            scratch(*upward.shape),
            scratch(*child_ops.shape, dtype=jnp.bfloat16),
            scratch(steps, channels, batch * channels, dtype=jnp.bfloat16),
            scratch(GRID * GRID, rows, blocks),
            scratch(GRID, rows, blocks),
            scratch(4, rows, blocks),
            *[scratch(2 * part, blocks) for part in parts],
            *[scratch(devices, 1, width) for width in widths * 2],
            scratch(2, 3, channels, leaf_count, dtype=jnp.bfloat16),
            scratch(batch * channels, leaf_count, dtype=jnp.bfloat16),
            pltpu.SemaphoreType.DMA((9,)),
            pltpu.SemaphoreType.DMA((steps,)),
            pltpu.SemaphoreType.DMA((2,)),
            pltpu.SemaphoreType.DMA((2,)),
            pltpu.SemaphoreType.DMA((5,)),
            pltpu.SemaphoreType.DMA((5,)),
        ],
        compiler_params=pltpu.CompilerParams(
            vmem_limit_bytes=56 << 20, has_side_effects=True, collective_id=0
        ),
        name="step",
    )(
        table,
        positions,
        charges,
        counts.reshape(1, blocks),
        owners.reshape(1, blocks),
        leaves.reshape(1, blocks),
        near_lists,
        image_lists,
        upward,
        child_ops,
        direct_ops.T,
        image_ops.T,
    )
    return (potentials[:, None, :], parents.T[:, None, :])


def solution(mesh):
    return jax.shard_map(
        local,
        mesh=mesh,
        in_specs=(
            P(None, ("box", "depth"), None),
            P(None, ("box", "depth"), None),
            P(("box", "depth")),
            P(("box", "depth"), None),
            P(("box", "depth")),
            P(None, "depth", "box"),
            P(None, "depth", "box"),
            P(),
            P(),
            P(),
            P(),
        ),
        out_specs=(P(None, "depth", "box"), P(None, "depth", "box")),
        check_vma=False,
    )
```

```python
import functools

import jax
import jax.numpy as jnp
import numpy as np
from jax import lax
from jax.experimental import pallas as pl
from jax.experimental.pallas import tpu as pltpu
from jax.sharding import PartitionSpec as P
from numpy.polynomial import chebyshev, polynomial

GRID = 6
VM = pl.BlockSpec(memory_space=pltpu.VMEM)
HBM = pl.BlockSpec(memory_space=pltpu.HBM)
SM = pl.BlockSpec(memory_space=pltpu.SMEM)


def surface_index(grid_size):
    indices = np.arange(grid_size)
    lattice = np.stack(np.meshgrid(indices, indices, indices, indexing="ij"), -1).reshape(-1, 3)
    outside = np.any((lattice == 0) | (lattice == grid_size - 1), axis=1)
    return lattice[outside].astype(np.int32)


def node_coordinates(grid_size):
    middle = (grid_size - 1) / 2.0
    return ((np.arange(grid_size) - middle) * (1.5 / middle)).astype(np.float32)


def series(function, degree):
    fitted = chebyshev.Chebyshev.interpolate(function, degree, domain=[1.0, 12.0])
    return [float(value) for value in fitted.convert(kind=polynomial.Polynomial).coef]


HALF_SINE = series(lambda s: np.sin(np.sqrt(s) / 2) / (np.sqrt(s) / 2), 4)
HALF_COSINE = series(lambda s: np.cos(np.sqrt(s) / 2), 5)


SCALE = 2.0 * HALF_SINE[-1] * HALF_COSINE[-1]


def monic(coefficients, s):
    value = s + coefficients[-2] / coefficients[-1]
    for coefficient in coefficients[-3::-1]:
        value = value * s + coefficient / coefficients[-1]
    return value


def waves(s):
    sine = monic(HALF_SINE, s)
    cosine = monic(HALF_COSINE, s)
    sine = sine * cosine
    cosine = cosine * cosine * (2.0 * HALF_COSINE[-1] ** 2) - 1.0
    return (cosine * cosine - 0.5) * lax.rsqrt(s), sine * cosine


def pieces(value, count=3):
    terms = []
    for _ in range(count):
        terms.append(value.astype(jnp.bfloat16))
        value = value - terms[-1].astype(jnp.float32)
    return terms


def prepare_sources(positions, charges, counts, planes, depths, live_charges):
    nodes = node_coordinates(GRID)
    blocks, rows = positions.shape[1:]
    x, y, z = positions[0].T, positions[1].T, positions[2].T
    squares = []
    for node in nodes:
        delta = float(node) - y
        squares.append(delta * delta)
    for i, node in enumerate(nodes):
        delta = float(node) - x
        delta = delta * delta
        for j in range(len(nodes)):
            planes[i * len(nodes) + j] = delta + squares[j]
        delta = float(node) - z
        depths[i] = delta * delta
    live = lax.broadcasted_iota(jnp.int32, (rows, blocks), 0) < counts[...]
    for part in range(2):
        charge = jnp.where(live, charges[part].T, 0.0)
        live_charges[part] = 2.0 * charge
        live_charges[2 + part] = SCALE * charge


def sum_point(table, planes, depths, live_charges, values, first, p):
    plane = table[0, first + p]
    depth = table[1, first + p]
    real = imaginary = None
    for chunk in range(planes.shape[1] // 8):
        place = pl.ds(8 * chunk, 8)
        cosine, sine = waves(planes[plane, place, :] + depths[depth, place, :])
        a = cosine * live_charges[0, place, :] - sine * live_charges[3, place, :]
        b = sine * live_charges[2, place, :] + cosine * live_charges[1, place, :]
        real = a if real is None else real + a
        imaginary = b if imaginary is None else imaginary + b
    values[pl.ds(p, 1), :] = jnp.sum(real, axis=0, keepdims=True)
    values[pl.ds(values.shape[0] // 2 + p, 1), :] = jnp.sum(imaginary, axis=0, keepdims=True)


def ranks(owners):
    blocks = owners.shape[1]
    shape = (blocks, blocks)
    target = jnp.broadcast_to(owners[...].astype(jnp.float32), shape)
    earlier = (target == target.T) & (
        lax.broadcasted_iota(jnp.int32, shape, 0) < lax.broadcasted_iota(jnp.int32, shape, 1)
    )
    return jnp.sum(jnp.where(earlier, 1.0, 0.0), axis=0, keepdims=True)


def fill_slots(values, owners, rank, leaves, sent, capacity):
    devices, _, width = sent.shape
    channels, blocks = values.shape
    device = lax.broadcasted_iota(jnp.int32, (devices, blocks), 0)
    spare = width - capacity * channels
    place_row = lax.broadcasted_iota(jnp.int32, (spare, blocks), 0)
    leaf = jnp.broadcast_to(leaves[...].astype(jnp.float32), (spare, blocks))
    filled = None
    for place in range(capacity):
        pick = jnp.where((device == owners[...]) & (rank == place), 1.0, 0.0).astype(jnp.bfloat16)
        column = jnp.concatenate(
            [
                values[...] if other == place else jnp.zeros((channels, blocks), jnp.float32)
                for other in range(capacity)
            ]
            + [jnp.where(place_row == place, leaf, 0.0)],
            axis=0,
        )
        for term in pieces(column):
            part = lax.dot_general(
                pick, term, (((1,), (1,)), ((), ())), preferred_element_type=jnp.float32
            )
            filled = part if filled is None else filled + part
    sent[:, 0, :] = filled


def raise_part(arrived, upward, capacity, first, count):
    rows = arrived[:, 0, :]
    channels = 2 * count
    values = jnp.concatenate(
        [rows[:, place * channels : (place + 1) * channels] for place in range(capacity)], axis=0
    )
    points = upward.shape[1] // 2
    columns = jnp.concatenate(
        [upward[:, first : first + count], upward[:, points + first : points + first + count]],
        axis=1,
    )
    return lax.dot_general(
        columns,
        values,
        (((1,), (1,)), ((), ())),
        precision=lax.Precision.HIGHEST,
        preferred_element_type=jnp.float32,
    )


def add_up(raised, arrived, capacity, count, leaf_count):
    rows = arrived[:, 0, :]
    first = capacity * 2 * count
    leaf = jnp.concatenate(
        [rows[:, first + place : first + place + 1] for place in range(capacity)], axis=0
    ).astype(jnp.int32)
    members = jnp.where(
        lax.broadcasted_iota(jnp.int32, (leaf.shape[0], leaf_count), 1) == leaf, 1.0, 0.0
    ).astype(jnp.bfloat16)
    summed = sum(
        jnp.dot(term, members, preferred_element_type=jnp.float32) for term in pieces(raised)
    )
    return summed.astype(jnp.bfloat16)


def parents_of(multipole, child_ops):
    channels, leaf_count = multipole.shape
    family = child_ops.shape[1] // channels
    wide = jnp.broadcast_to(
        multipole.astype(jnp.float32)[:, None, :], (channels, family, leaf_count)
    )
    shape = (channels, family, leaf_count)
    mine = lax.broadcasted_iota(jnp.int32, shape, 2) % family == lax.broadcasted_iota(
        jnp.int32, shape, 1
    )
    children = jnp.where(mine, wide, 0.0).reshape(channels * family, leaf_count)
    spread = jnp.dot(
        child_ops[...], children.astype(jnp.bfloat16), preferred_element_type=jnp.float32
    )
    shape = (leaf_count // family, leaf_count)
    group = jnp.where(
        lax.broadcasted_iota(jnp.int32, shape, 1) // family
        == lax.broadcasted_iota(jnp.int32, shape, 0),
        1.0,
        0.0,
    ).astype(jnp.bfloat16)
    return sum(
        lax.dot_general(group, term, (((1,), (1,)), ((), ())), preferred_element_type=jnp.float32)
        for term in pieces(spread)
    )


def step_kernel(
    table,
    positions_in,
    charges_in,
    counts_in,
    owners_in,
    leaves_in,
    near_in,
    image_in,
    upward_in,
    child_in,
    direct_in,
    mirrored_in,
    potentials,
    parents,
    positions,
    charges,
    counts,
    owners,
    leaves,
    lists,
    upward,
    child_ops,
    operators,
    planes,
    depths,
    live_charges,
    early_values,
    late_values,
    early_sent,
    late_sent,
    early_arrived,
    late_arrived,
    windows,
    gathered,
    input_sem,
    operator_sem,
    send_sem,
    arrive_sem,
    halo_send,
    halo_recv,
):
    box, depth = lax.axis_index("box"), lax.axis_index("depth")
    boxes, slabs = lax.axis_size("box"), lax.axis_size("depth")
    devices = early_sent.shape[0]
    early, late = early_values.shape[0] // 2, late_values.shape[0] // 2
    channels, leaf_count = potentials.shape
    capacity = early_sent.shape[2] // (2 * early)
    offsets = near_in.shape[0]
    steps, _, width = operators.shape
    batch = width // channels
    half = steps // 2
    me = box * slabs + depth

    fetches = [
        pltpu.make_async_copy(source, place, input_sem.at[number])
        for number, (source, place) in enumerate(
            [
                (positions_in, positions),
                (charges_in, charges),
                (counts_in, counts),
                (owners_in, owners),
                (leaves_in, leaves),
                (near_in, lists.at[pl.ds(0, offsets)]),
                (image_in, lists.at[pl.ds(offsets, offsets)]),
                (upward_in, upward),
                (child_in, child_ops),
            ]
        )
    ]
    for fetch in fetches[:5]:
        fetch.start()
    barrier = pltpu.get_barrier_semaphore()
    columns = [lax.rem(depth + ahead, slabs) for ahead in range(slabs)]

    def own_row(send):
        for column in columns[1:]:
            send(box, column)

    def one_row(ahead, send):
        target_box = lax.rem(box + ahead, boxes)
        for column in columns:
            send(target_box, column)

    def other_rows(send):
        def body(ahead, carry):
            one_row(ahead, send)
            return carry

        lax.fori_loop(1, boxes, body, 0)

    def greet(target_box, target_depth):
        pl.semaphore_signal(
            barrier,
            inc=1,
            device_id=(target_box, target_depth),
            device_id_type=pl.DeviceIdType.MESH,
        )

    own_row(greet)
    other_rows(greet)
    for fetch in fetches[:5]:
        fetch.wait()
    for fetch in fetches[5:]:
        fetch.start()
    for step in range(steps):
        pltpu.make_async_copy(
            (direct_in if step < half else mirrored_in).at[
                :, pl.ds(step % half * width, width)
            ],
            operators.at[step],
            operator_sem.at[step],
        ).start()
    prepare_sources(positions, charges, counts, planes, depths, live_charges)
    rank = ranks(owners)

    def early_point(p, carry):
        sum_point(table, planes, depths, live_charges, early_values, 0, p)
        return carry

    lax.fori_loop(0, early, early_point, 0, unroll=4)
    fill_slots(early_values, owners, rank, leaves, early_sent, capacity)
    pl.semaphore_wait(barrier, devices - 1)

    def route(number, sent, arrived):
        def send(target_box, target_depth):
            pltpu.make_async_remote_copy(
                src_ref=sent.at[target_box * slabs + target_depth],
                dst_ref=arrived.at[me],
                send_sem=send_sem.at[number],
                recv_sem=arrive_sem.at[number],
                device_id=(target_box, target_depth),
                device_id_type=pl.DeviceIdType.MESH,
            ).start()

        return send

    def all_routed(number, sent, arrived):
        others = pl.ds(0, devices - 1)
        return pltpu.make_async_remote_copy(
            src_ref=sent.at[others],
            dst_ref=arrived.at[others],
            send_sem=send_sem.at[number],
            recv_sem=arrive_sem.at[number],
            device_id=(lax.rem(box + 1, boxes), depth),
            device_id_type=pl.DeviceIdType.MESH,
        )

    early_send = route(0, early_sent, early_arrived)
    late_send = route(1, late_sent, late_arrived)
    early_all = all_routed(0, early_sent, early_arrived)
    late_all = all_routed(1, late_sent, late_arrived)
    own_row(early_send)

    def late_points(pair):
        for p in range(2):
            sum_point(table, planes, depths, live_charges, late_values, early, 2 * pair + p)

    def late_and_send(pair, carry):
        late_points(pair)
        one_row(pair + 1, early_send)
        return carry

    def late_only(pair, carry):
        late_points(pair)
        return carry

    lax.fori_loop(0, boxes - 1, late_and_send, 0)
    lax.fori_loop(boxes - 1, late // 2, late_only, 0)
    fill_slots(late_values, owners, rank, leaves, late_sent, capacity)
    own_row(late_send)
    other_rows(late_send)
    early_arrived[me] = early_sent[me]
    late_arrived[me] = late_sent[me]
    for fetch in fetches[5:]:
        fetch.wait()
    early_all.wait_recv()
    raised = raise_part(early_arrived, upward, capacity, 0, early)
    late_all.wait_recv()
    raised += raise_part(late_arrived, upward, capacity, early, late)
    windows[0, 1] = add_up(raised, late_arrived, capacity, late, leaf_count)

    def copy(number, source, place, device):
        return pltpu.make_async_remote_copy(
            src_ref=windows.at[source],
            dst_ref=windows.at[place],
            send_sem=halo_send.at[number],
            recv_sem=halo_recv.at[number],
            device_id=device,
            device_id_type=pl.DeviceIdType.MESH,
        )

    def beside(number, slab):
        to_right = copy(number, (slab, 1), (slab, 0), (box + 1, depth))
        to_left = copy(number + 1, (slab, 1), (slab, 2), (box - 1, depth))
        return to_right, to_left

    mirror = copy(4, (0, 1), (1, 1), (box, slabs - 1 - depth))
    direct, image = beside(0, 0), beside(2, 1)
    has_left, has_right = box > 0, box < boxes - 1
    blank = jnp.zeros((channels, leaf_count), jnp.bfloat16)

    def start(pair):
        @pl.when(has_right)
        def _():
            pair[0].start()

        @pl.when(has_left)
        def _():
            pair[1].start()

    def receive(pair):
        @pl.when(has_left)
        def _():
            pair[0].wait_recv()

        @pl.when(has_right)
        def _():
            pair[1].wait_recv()

    def sent_off(pair):
        @pl.when(has_right)
        def _():
            pair[0].wait_send()

        @pl.when(has_left)
        def _():
            pair[1].wait_send()

    start(direct)
    mirror.start()

    @pl.when(jnp.logical_not(has_left))
    def _():
        windows[0, 0] = blank
        windows[1, 0] = blank

    @pl.when(jnp.logical_not(has_right))
    def _():
        windows[0, 2] = blank
        windows[1, 2] = blank

    parents[...] = parents_of(windows[0, 1], child_ops)
    potentials[...] = jnp.zeros_like(potentials)
    row = lax.broadcasted_iota(jnp.int32, (leaf_count, leaf_count), 0)

    def one_hot(number, parts):
        chosen = lists[number]
        return jnp.concatenate(
            [
                jnp.where(row == chosen - part * leaf_count, 1.0, 0.0).astype(jnp.bfloat16)
                for part in parts
            ],
            axis=0,
        )

    def gather(window, number, parts):
        picked = jnp.dot(window, one_hot(number, parts), preferred_element_type=jnp.float32)
        return picked.astype(jnp.bfloat16)

    def place_of(offset):
        return pl.ds(pl.multiple_of(offset * channels, 16), channels)

    def operate(step):
        pltpu.make_async_copy(
            direct_in.at[:, pl.ds(0, width)], operators.at[step], operator_sem.at[step]
        ).wait()
        rows = pl.ds(pl.multiple_of(lax.rem(step, half) * width, 16), width)
        potentials[...] += jnp.dot(
            operators[step], gathered[rows, :], preferred_element_type=jnp.float32
        )

    def own_part(step, carry):
        for o in range(batch // 2):
            offset = step * (batch // 2) + o
            gathered[place_of(offset), :] = gather(windows[0, 1], offset, (1,))
        return carry

    lax.fori_loop(0, 2 * half, own_part, 0)
    receive(direct)

    def direct_step(step, carry):
        @pl.when(step == half // 2)
        def _():
            mirror.wait_recv()
            start(image)

        window = jnp.concatenate([windows[0, 0], windows[0, 2]], axis=1)
        for o in range(batch):
            offset = step * batch + o
            gathered[place_of(offset), :] += gather(window, offset, (0, 2))
        operate(step)
        return carry

    lax.fori_loop(0, half, direct_step, 0)
    receive(image)

    def image_step(step, carry):
        window = jnp.concatenate([windows[1, part] for part in range(3)], axis=1)
        for o in range(batch):
            offset = (step - half) * batch + o
            gathered[place_of(offset), :] = gather(window, offsets + offset, (0, 1, 2))
        operate(step)
        return carry

    lax.fori_loop(half, steps, image_step, 0)
    early_all.wait_send()
    late_all.wait_send()
    sent_off(direct)
    sent_off(image)
    mirror.wait_send()


def hand_over_kernel(potentials, parents, potentials_out, parents_out):
    potentials_out[:, 0, :] = potentials[...]
    parents_out[...] = parents[...]


def local(
    positions,
    charges,
    counts,
    owners,
    leaves,
    near_lists,
    image_lists,
    upward,
    child_ops,
    direct_ops,
    image_ops,
):
    devices = lax.axis_size("box") * lax.axis_size("depth")
    blocks, rows = positions.shape[1:]
    capacity = 2 * blocks // devices
    offsets, _, leaf_count = near_lists.shape
    channels = upward.shape[0]
    index = surface_index(GRID)
    table = jnp.asarray(np.stack([index[:, 0] * GRID + index[:, 1], index[:, 2]]))
    batch = 32
    steps = 2 * offsets // batch
    points = channels // 2
    early = points * 11 // 16 // 8 * 8
    parts = (early, points - early)
    widths = [-(-capacity * (2 * part + 1) // 128) * 128 for part in parts]
    parent_count = leaf_count * channels // child_ops.shape[1]

    def scratch(*shape, dtype=jnp.float32):
        return pltpu.VMEM(shape, dtype)

    potentials, parents = pl.pallas_call(
        step_kernel,
        out_shape=(
            jax.ShapeDtypeStruct((channels, leaf_count), jnp.float32),
            jax.ShapeDtypeStruct((parent_count, channels), jnp.float32),
        ),
        in_specs=[SM] + [HBM] * 11,
        out_specs=(VM, VM),
        scratch_shapes=[
            scratch(*positions.shape),
            scratch(*charges.shape),
            scratch(1, blocks, dtype=jnp.int32),
            scratch(1, blocks, dtype=jnp.int32),
            scratch(1, blocks, dtype=jnp.int32),
            scratch(2 * offsets, 1, leaf_count, dtype=jnp.int32),
            scratch(*upward.shape),
            scratch(*child_ops.shape, dtype=jnp.bfloat16),
            scratch(steps, channels, batch * channels, dtype=jnp.bfloat16),
            scratch(GRID * GRID, rows, blocks),
            scratch(GRID, rows, blocks),
            scratch(4, rows, blocks),
            *[scratch(2 * part, blocks) for part in parts],
            *[scratch(devices, 1, width) for width in widths * 2],
            scratch(2, 3, channels, leaf_count, dtype=jnp.bfloat16),
            scratch(offsets * channels, leaf_count, dtype=jnp.bfloat16),
            pltpu.SemaphoreType.DMA((9,)),
            pltpu.SemaphoreType.DMA((steps,)),
            pltpu.SemaphoreType.DMA((2,)),
            pltpu.SemaphoreType.DMA((2,)),
            pltpu.SemaphoreType.DMA((5,)),
            pltpu.SemaphoreType.DMA((5,)),
        ],
        compiler_params=pltpu.CompilerParams(
            vmem_limit_bytes=56 << 20, has_side_effects=True, collective_id=0
        ),
        name="step",
    )(
        table,
        positions,
        charges,
        counts.reshape(1, blocks),
        owners.reshape(1, blocks),
        leaves.reshape(1, blocks),
        near_lists,
        image_lists,
        upward,
        child_ops,
        direct_ops.T,
        image_ops.T,
    )
    potentials, parents = pl.pallas_call(
        hand_over_kernel,
        out_shape=(
            jax.ShapeDtypeStruct((channels, 1, leaf_count), jnp.float32),
            jax.ShapeDtypeStruct((parent_count, channels), jnp.float32),
        ),
        in_specs=[VM, VM],
        out_specs=(VM, VM),
        name="hand_over",
    )(potentials, parents)
    return (potentials, parents.T[:, None, :])


def solution(mesh):
    return jax.shard_map(
        local,
        mesh=mesh,
        in_specs=(
            P(None, ("box", "depth"), None),
            P(None, ("box", "depth"), None),
            P(("box", "depth")),
            P(("box", "depth"), None),
            P(("box", "depth")),
            P(None, "depth", "box"),
            P(None, "depth", "box"),
            P(),
            P(),
            P(),
            P(),
        ),
        out_specs=(P(None, "depth", "box"), P(None, "depth", "box")),
        check_vma=False,
    )
```

```python
import functools

import jax
import jax.numpy as jnp
import numpy as np
from jax import lax
from jax.experimental import pallas as pl
from jax.experimental.pallas import tpu as pltpu
from jax.sharding import PartitionSpec as P
from numpy.polynomial import chebyshev, polynomial

GRID = 6
VM = pl.BlockSpec(memory_space=pltpu.VMEM)
HBM = pl.BlockSpec(memory_space=pltpu.HBM)
SM = pl.BlockSpec(memory_space=pltpu.SMEM)


def surface_index(grid_size):
    indices = np.arange(grid_size)
    lattice = np.stack(np.meshgrid(indices, indices, indices, indexing="ij"), -1).reshape(-1, 3)
    outside = np.any((lattice == 0) | (lattice == grid_size - 1), axis=1)
    return lattice[outside].astype(np.int32)


def node_coordinates(grid_size):
    middle = (grid_size - 1) / 2.0
    return ((np.arange(grid_size) - middle) * (1.5 / middle)).astype(np.float32)


def series(function, degree):
    fitted = chebyshev.Chebyshev.interpolate(function, degree, domain=[1.0, 12.0])
    return [float(value) for value in fitted.convert(kind=polynomial.Polynomial).coef]


HALF_SINE = series(lambda s: np.sin(np.sqrt(s) / 2) / (np.sqrt(s) / 2), 4)
HALF_COSINE = series(lambda s: np.cos(np.sqrt(s) / 2), 5)


SCALE = 2.0 * HALF_SINE[-1] * HALF_COSINE[-1]


def monic(coefficients, s):
    value = s + coefficients[-2] / coefficients[-1]
    for coefficient in coefficients[-3::-1]:
        value = value * s + coefficient / coefficients[-1]
    return value


def waves(s):
    sine = monic(HALF_SINE, s)
    cosine = monic(HALF_COSINE, s)
    sine = sine * cosine
    cosine = cosine * cosine * (2.0 * HALF_COSINE[-1] ** 2) - 1.0
    return (cosine * cosine - 0.5) * lax.rsqrt(s), sine * cosine


def pieces(value, count=3):
    terms = []
    for _ in range(count):
        terms.append(value.astype(jnp.bfloat16))
        value = value - terms[-1].astype(jnp.float32)
    return terms


def prepare_sources(positions, charges, counts, planes, depths, live_charges):
    nodes = node_coordinates(GRID)
    blocks, rows = positions.shape[1:]
    x, y, z = positions[0].T, positions[1].T, positions[2].T
    squares = []
    for node in nodes:
        delta = float(node) - y
        squares.append(delta * delta)
    for i, node in enumerate(nodes):
        delta = float(node) - x
        delta = delta * delta
        for j in range(len(nodes)):
            planes[i * len(nodes) + j] = delta + squares[j]
        delta = float(node) - z
        depths[i] = delta * delta
    live = lax.broadcasted_iota(jnp.int32, (rows, blocks), 0) < counts[...]
    for part in range(2):
        charge = jnp.where(live, charges[part].T, 0.0)
        live_charges[part] = 2.0 * charge
        live_charges[2 + part] = SCALE * charge


def sum_point(table, planes, depths, live_charges, values, first, p):
    plane = table[0, first + p]
    depth = table[1, first + p]
    real = imaginary = None
    for chunk in range(planes.shape[1] // 8):
        place = pl.ds(8 * chunk, 8)
        cosine, sine = waves(planes[plane, place, :] + depths[depth, place, :])
        a = cosine * live_charges[0, place, :] - sine * live_charges[3, place, :]
        b = sine * live_charges[2, place, :] + cosine * live_charges[1, place, :]
        real = a if real is None else real + a
        imaginary = b if imaginary is None else imaginary + b
    values[pl.ds(p, 1), :] = jnp.sum(real, axis=0, keepdims=True)
    values[pl.ds(values.shape[0] // 2 + p, 1), :] = jnp.sum(imaginary, axis=0, keepdims=True)


def ranks(owners):
    blocks = owners.shape[1]
    shape = (blocks, blocks)
    target = jnp.broadcast_to(owners[...].astype(jnp.float32), shape)
    earlier = (target == target.T) & (
        lax.broadcasted_iota(jnp.int32, shape, 0) < lax.broadcasted_iota(jnp.int32, shape, 1)
    )
    return jnp.sum(jnp.where(earlier, 1.0, 0.0), axis=0, keepdims=True)


def fill_slots(values, owners, rank, leaves, sent, capacity):
    devices, _, width = sent.shape
    channels, blocks = values.shape
    device = lax.broadcasted_iota(jnp.int32, (devices, blocks), 0)
    spare = width - capacity * channels
    place_row = lax.broadcasted_iota(jnp.int32, (spare, blocks), 0)
    leaf = jnp.broadcast_to(leaves[...].astype(jnp.float32), (spare, blocks))
    filled = None
    for place in range(capacity):
        pick = jnp.where((device == owners[...]) & (rank == place), 1.0, 0.0).astype(jnp.bfloat16)
        column = jnp.concatenate(
            [
                values[...] if other == place else jnp.zeros((channels, blocks), jnp.float32)
                for other in range(capacity)
            ]
            + [jnp.where(place_row == place, leaf, 0.0)],
            axis=0,
        )
        for term in pieces(column):
            part = lax.dot_general(
                pick, term, (((1,), (1,)), ((), ())), preferred_element_type=jnp.float32
            )
            filled = part if filled is None else filled + part
    sent[:, 0, :] = filled


def raise_part(arrived, upward, capacity, first, count):
    rows = arrived[:, 0, :]
    channels = 2 * count
    values = jnp.concatenate(
        [rows[:, place * channels : (place + 1) * channels] for place in range(capacity)], axis=0
    )
    points = upward.shape[1] // 2
    columns = jnp.concatenate(
        [upward[:, first : first + count], upward[:, points + first : points + first + count]],
        axis=1,
    )
    return lax.dot_general(
        columns,
        values,
        (((1,), (1,)), ((), ())),
        precision=lax.Precision.HIGHEST,
        preferred_element_type=jnp.float32,
    )


def add_up(raised, arrived, capacity, count, leaf_count):
    rows = arrived[:, 0, :]
    first = capacity * 2 * count
    leaf = jnp.concatenate(
        [rows[:, first + place : first + place + 1] for place in range(capacity)], axis=0
    ).astype(jnp.int32)
    members = jnp.where(
        lax.broadcasted_iota(jnp.int32, (leaf.shape[0], leaf_count), 1) == leaf, 1.0, 0.0
    ).astype(jnp.bfloat16)
    summed = sum(
        jnp.dot(term, members, preferred_element_type=jnp.float32) for term in pieces(raised)
    )
    return summed.astype(jnp.bfloat16)


def parents_of(multipole, child_ops):
    channels, leaf_count = multipole.shape
    family = child_ops.shape[1] // channels
    wide = jnp.broadcast_to(
        multipole.astype(jnp.float32)[:, None, :], (channels, family, leaf_count)
    )
    shape = (channels, family, leaf_count)
    mine = lax.broadcasted_iota(jnp.int32, shape, 2) % family == lax.broadcasted_iota(
        jnp.int32, shape, 1
    )
    children = jnp.where(mine, wide, 0.0).reshape(channels * family, leaf_count)
    spread = jnp.dot(
        child_ops[...], children.astype(jnp.bfloat16), preferred_element_type=jnp.float32
    )
    shape = (leaf_count // family, leaf_count)
    group = jnp.where(
        lax.broadcasted_iota(jnp.int32, shape, 1) // family
        == lax.broadcasted_iota(jnp.int32, shape, 0),
        1.0,
        0.0,
    ).astype(jnp.bfloat16)
    return sum(
        lax.dot_general(group, term, (((1,), (1,)), ((), ())), preferred_element_type=jnp.float32)
        for term in pieces(spread)
    )


def step_kernel(
    table,
    positions_in,
    charges_in,
    counts_in,
    owners_in,
    leaves_in,
    near_in,
    image_in,
    upward_in,
    child_in,
    direct_in,
    mirrored_in,
    potentials,
    parents,
    positions,
    charges,
    counts,
    owners,
    leaves,
    lists,
    upward,
    child_ops,
    operators,
    planes,
    depths,
    live_charges,
    early_values,
    late_values,
    early_sent,
    late_sent,
    early_arrived,
    late_arrived,
    windows,
    gathered,
    input_sem,
    operator_sem,
    send_sem,
    arrive_sem,
    halo_send,
    halo_recv,
):
    box, depth = lax.axis_index("box"), lax.axis_index("depth")
    boxes, slabs = lax.axis_size("box"), lax.axis_size("depth")
    devices = early_sent.shape[0]
    early, late = early_values.shape[0] // 2, late_values.shape[0] // 2
    channels, leaf_count = potentials.shape
    capacity = early_sent.shape[2] // (2 * early)
    offsets = near_in.shape[0]
    steps, _, width = operators.shape
    batch = width // channels
    half = steps // 2
    me = box * slabs + depth

    fetches = [
        pltpu.make_async_copy(source, place, input_sem.at[number])
        for number, (source, place) in enumerate(
            [
                (positions_in, positions),
                (charges_in, charges),
                (counts_in, counts),
                (owners_in, owners),
                (leaves_in, leaves),
                (near_in, lists.at[pl.ds(0, offsets)]),
                (image_in, lists.at[pl.ds(offsets, offsets)]),
                (upward_in, upward),
                (child_in, child_ops),
            ]
        )
    ]
    for fetch in fetches[:5]:
        fetch.start()
    barrier = pltpu.get_barrier_semaphore()
    columns = [lax.rem(depth + ahead, slabs) for ahead in range(slabs)]

    def own_row(send):
        for column in columns[1:]:
            send(box, column)

    def one_row(ahead, send):
        target_box = lax.rem(box + ahead, boxes)
        for column in columns:
            send(target_box, column)

    def other_rows(send):
        def body(ahead, carry):
            one_row(ahead, send)
            return carry

        lax.fori_loop(1, boxes, body, 0)

    def greet(target_box, target_depth):
        pl.semaphore_signal(
            barrier,
            inc=1,
            device_id=(target_box, target_depth),
            device_id_type=pl.DeviceIdType.MESH,
        )

    own_row(greet)
    other_rows(greet)
    for fetch in fetches[:5]:
        fetch.wait()
    for fetch in fetches[5:]:
        fetch.start()
    for step in range(steps):
        pltpu.make_async_copy(
            (direct_in if step < half else mirrored_in).at[
                :, pl.ds(step % half * width, width)
            ],
            operators.at[step],
            operator_sem.at[step],
        ).start()
    prepare_sources(positions, charges, counts, planes, depths, live_charges)
    rank = ranks(owners)

    def early_point(p, carry):
        sum_point(table, planes, depths, live_charges, early_values, 0, p)
        return carry

    lax.fori_loop(0, early, early_point, 0, unroll=4)
    fill_slots(early_values, owners, rank, leaves, early_sent, capacity)
    pl.semaphore_wait(barrier, devices - 1)

    def route(number, sent, arrived):
        def send(target_box, target_depth):
            pltpu.make_async_remote_copy(
                src_ref=sent.at[target_box * slabs + target_depth],
                dst_ref=arrived.at[me],
                send_sem=send_sem.at[number],
                recv_sem=arrive_sem.at[number],
                device_id=(target_box, target_depth),
                device_id_type=pl.DeviceIdType.MESH,
            ).start()

        return send

    def all_routed(number, sent, arrived):
        others = pl.ds(0, devices - 1)
        return pltpu.make_async_remote_copy(
            src_ref=sent.at[others],
            dst_ref=arrived.at[others],
            send_sem=send_sem.at[number],
            recv_sem=arrive_sem.at[number],
            device_id=(lax.rem(box + 1, boxes), depth),
            device_id_type=pl.DeviceIdType.MESH,
        )

    early_send = route(0, early_sent, early_arrived)
    late_send = route(1, late_sent, late_arrived)
    early_all = all_routed(0, early_sent, early_arrived)
    late_all = all_routed(1, late_sent, late_arrived)
    own_row(early_send)

    def late_points(pair):
        for p in range(2):
            sum_point(table, planes, depths, live_charges, late_values, early, 2 * pair + p)

    def late_and_send(pair, carry):
        late_points(pair)
        one_row(pair + 1, early_send)
        return carry

    def late_only(pair, carry):
        late_points(pair)
        return carry

    lax.fori_loop(0, boxes - 1, late_and_send, 0)
    lax.fori_loop(boxes - 1, late // 2, late_only, 0)
    fill_slots(late_values, owners, rank, leaves, late_sent, capacity)
    own_row(late_send)
    other_rows(late_send)
    early_arrived[me] = early_sent[me]
    late_arrived[me] = late_sent[me]
    for fetch in fetches[5:]:
        fetch.wait()
    early_all.wait_recv()
    raised = raise_part(early_arrived, upward, capacity, 0, early)
    late_all.wait_recv()
    raised += raise_part(late_arrived, upward, capacity, early, late)
    windows[0, 1] = add_up(raised, late_arrived, capacity, late, leaf_count)

    def copy(number, source, place, device):
        return pltpu.make_async_remote_copy(
            src_ref=windows.at[source],
            dst_ref=windows.at[place],
            send_sem=halo_send.at[number],
            recv_sem=halo_recv.at[number],
            device_id=device,
            device_id_type=pl.DeviceIdType.MESH,
        )

    def beside(number, slab):
        to_right = copy(number, (slab, 1), (slab, 0), (box + 1, depth))
        to_left = copy(number + 1, (slab, 1), (slab, 2), (box - 1, depth))
        return to_right, to_left

    mirror = copy(4, (0, 1), (1, 1), (box, slabs - 1 - depth))
    direct, image = beside(0, 0), beside(2, 1)
    has_left, has_right = box > 0, box < boxes - 1
    blank = jnp.zeros((channels, leaf_count), jnp.bfloat16)

    def start(pair):
        @pl.when(has_right)
        def _():
            pair[0].start()

        @pl.when(has_left)
        def _():
            pair[1].start()

    def receive(pair):
        @pl.when(has_left)
        def _():
            pair[0].wait_recv()

        @pl.when(has_right)
        def _():
            pair[1].wait_recv()

    def sent_off(pair):
        @pl.when(has_right)
        def _():
            pair[0].wait_send()

        @pl.when(has_left)
        def _():
            pair[1].wait_send()

    start(direct)

    @pl.when(jnp.logical_not(has_left))
    def _():
        windows[0, 0] = blank
        windows[1, 0] = blank

    @pl.when(jnp.logical_not(has_right))
    def _():
        windows[0, 2] = blank
        windows[1, 2] = blank

    parents[...] = parents_of(windows[0, 1], child_ops)
    potentials[...] = jnp.zeros_like(potentials)
    receive(direct)
    mirror.start()
    row = lax.broadcasted_iota(jnp.int32, (leaf_count, leaf_count), 0)

    def translate(step, carry):
        @pl.when(step == half // 2)
        def _():
            mirror.wait_recv()
            start(image)

        @pl.when(step == half)
        def _():
            receive(image)

        pltpu.make_async_copy(
            direct_in.at[:, pl.ds(0, width)], operators.at[step], operator_sem.at[step]
        ).wait()
        slab = step // half
        window = jnp.concatenate([windows[slab, part] for part in range(3)], axis=1)
        for o in range(batch):
            chosen = lists[step * batch + o]
            hot = jnp.concatenate(
                [
                    jnp.where(row == chosen - part * leaf_count, 1.0, 0.0).astype(jnp.bfloat16)
                    for part in range(3)
                ],
                axis=0,
            )
            picked = jnp.dot(window, hot, preferred_element_type=jnp.float32)
            gathered[pl.ds(o * channels, channels), :] = picked.astype(jnp.bfloat16)
        potentials[...] += jnp.dot(
            operators[step], gathered[...], preferred_element_type=jnp.float32
        )
        return carry

    lax.fori_loop(0, steps, translate, 0)
    early_all.wait_send()
    late_all.wait_send()
    sent_off(direct)
    sent_off(image)
    mirror.wait_send()


def hand_over_kernel(potentials, parents, potentials_out, parents_out):
    potentials_out[:, 0, :] = potentials[...]
    parents_out[...] = parents[...]


def local(
    positions,
    charges,
    counts,
    owners,
    leaves,
    near_lists,
    image_lists,
    upward,
    child_ops,
    direct_ops,
    image_ops,
):
    devices = lax.axis_size("box") * lax.axis_size("depth")
    blocks, rows = positions.shape[1:]
    capacity = 2 * blocks // devices
    offsets, _, leaf_count = near_lists.shape
    channels = upward.shape[0]
    index = surface_index(GRID)
    table = jnp.asarray(np.stack([index[:, 0] * GRID + index[:, 1], index[:, 2]]))
    batch = 32
    steps = 2 * offsets // batch
    points = channels // 2
    early = points * 11 // 16 // 8 * 8
    parts = (early, points - early)
    widths = [-(-capacity * (2 * part + 1) // 128) * 128 for part in parts]
    parent_count = leaf_count * channels // child_ops.shape[1]

    def scratch(*shape, dtype=jnp.float32):
        return pltpu.VMEM(shape, dtype)

    potentials, parents = pl.pallas_call(
        step_kernel,
        out_shape=(
            jax.ShapeDtypeStruct((channels, leaf_count), jnp.float32),
            jax.ShapeDtypeStruct((parent_count, channels), jnp.float32),
        ),
        in_specs=[SM] + [HBM] * 11,
        out_specs=(VM, VM),
        scratch_shapes=[
            scratch(*positions.shape),
            scratch(*charges.shape),
            scratch(1, blocks, dtype=jnp.int32),
            scratch(1, blocks, dtype=jnp.int32),
            scratch(1, blocks, dtype=jnp.int32),
            scratch(2 * offsets, 1, leaf_count, dtype=jnp.int32),
            scratch(*upward.shape),
            scratch(*child_ops.shape, dtype=jnp.bfloat16),
            scratch(steps, channels, batch * channels, dtype=jnp.bfloat16),
            scratch(GRID * GRID, rows, blocks),
            scratch(GRID, rows, blocks),
            scratch(4, rows, blocks),
            *[scratch(2 * part, blocks) for part in parts],
            *[scratch(devices, 1, width) for width in widths * 2],
            scratch(2, 3, channels, leaf_count, dtype=jnp.bfloat16),
            scratch(batch * channels, leaf_count, dtype=jnp.bfloat16),
            pltpu.SemaphoreType.DMA((9,)),
            pltpu.SemaphoreType.DMA((steps,)),
            pltpu.SemaphoreType.DMA((2,)),
            pltpu.SemaphoreType.DMA((2,)),
            pltpu.SemaphoreType.DMA((5,)),
            pltpu.SemaphoreType.DMA((5,)),
        ],
        compiler_params=pltpu.CompilerParams(
            vmem_limit_bytes=56 << 20, has_side_effects=True, collective_id=0
        ),
        name="step",
    )(
        table,
        positions,
        charges,
        counts.reshape(1, blocks),
        owners.reshape(1, blocks),
        leaves.reshape(1, blocks),
        near_lists,
        image_lists,
        upward,
        child_ops,
        direct_ops.T,
        image_ops.T,
    )
    potentials, parents = pl.pallas_call(
        hand_over_kernel,
        out_shape=(
            jax.ShapeDtypeStruct((channels, 1, leaf_count), jnp.float32),
            jax.ShapeDtypeStruct((parent_count, channels), jnp.float32),
        ),
        in_specs=[VM, VM],
        out_specs=(VM, VM),
        name="hand_over",
    )(potentials, parents)
    return (potentials, parents.T[:, None, :])


def solution(mesh):
    return jax.shard_map(
        local,
        mesh=mesh,
        in_specs=(
            P(None, ("box", "depth"), None),
            P(None, ("box", "depth"), None),
            P(("box", "depth")),
            P(("box", "depth"), None),
            P(("box", "depth")),
            P(None, "depth", "box"),
            P(None, "depth", "box"),
            P(),
            P(),
            P(),
            P(),
        ),
        out_specs=(P(None, "depth", "box"), P(None, "depth", "box")),
        check_vma=False,
    )
```

```python
import functools

import jax
import jax.numpy as jnp
import numpy as np
from jax import lax
from jax.experimental import pallas as pl
from jax.experimental.pallas import tpu as pltpu
from jax.sharding import PartitionSpec as P
from numpy.polynomial import chebyshev, polynomial

GRID = 6
VM = pl.BlockSpec(memory_space=pltpu.VMEM)
HBM = pl.BlockSpec(memory_space=pltpu.HBM)
SM = pl.BlockSpec(memory_space=pltpu.SMEM)


def surface_index(grid_size):
    indices = np.arange(grid_size)
    lattice = np.stack(np.meshgrid(indices, indices, indices, indexing="ij"), -1).reshape(-1, 3)
    outside = np.any((lattice == 0) | (lattice == grid_size - 1), axis=1)
    return lattice[outside].astype(np.int32)


def node_coordinates(grid_size):
    middle = (grid_size - 1) / 2.0
    return ((np.arange(grid_size) - middle) * (1.5 / middle)).astype(np.float32)


def series(function, degree):
    fitted = chebyshev.Chebyshev.interpolate(function, degree, domain=[1.0, 12.0])
    return [float(value) for value in fitted.convert(kind=polynomial.Polynomial).coef]


HALF_SINE = series(lambda s: np.sin(np.sqrt(s) / 2) / (np.sqrt(s) / 2), 4)
HALF_COSINE = series(lambda s: np.cos(np.sqrt(s) / 2), 5)


SCALE = 2.0 * HALF_SINE[-1] * HALF_COSINE[-1]


def monic(coefficients, s):
    value = s + coefficients[-2] / coefficients[-1]
    for coefficient in coefficients[-3::-1]:
        value = value * s + coefficient / coefficients[-1]
    return value


def waves(s):
    sine = monic(HALF_SINE, s)
    cosine = monic(HALF_COSINE, s)
    sine = sine * cosine
    cosine = cosine * cosine * (2.0 * HALF_COSINE[-1] ** 2) - 1.0
    return (cosine * cosine - 0.5) * lax.rsqrt(s), sine * cosine


def pieces(value, count=3):
    terms = []
    for _ in range(count):
        terms.append(value.astype(jnp.bfloat16))
        value = value - terms[-1].astype(jnp.float32)
    return terms


def prepare_sources(positions, charges, counts, planes, depths, live_charges):
    nodes = node_coordinates(GRID)
    blocks, rows = positions.shape[1:]
    x, y, z = positions[0].T, positions[1].T, positions[2].T
    squares = []
    for node in nodes:
        delta = float(node) - y
        squares.append(delta * delta)
    for i, node in enumerate(nodes):
        delta = float(node) - x
        delta = delta * delta
        for j in range(len(nodes)):
            planes[i * len(nodes) + j] = delta + squares[j]
        delta = float(node) - z
        depths[i] = delta * delta
    live = lax.broadcasted_iota(jnp.int32, (rows, blocks), 0) < counts[...]
    for part in range(2):
        charge = jnp.where(live, charges[part].T, 0.0)
        live_charges[part] = 2.0 * charge
        live_charges[2 + part] = SCALE * charge


def sum_point(table, planes, depths, live_charges, values, first, p):
    plane = table[0, first + p]
    depth = table[1, first + p]
    real = imaginary = None
    for chunk in range(planes.shape[1] // 8):
        place = pl.ds(8 * chunk, 8)
        cosine, sine = waves(planes[plane, place, :] + depths[depth, place, :])
        a = cosine * live_charges[0, place, :] - sine * live_charges[3, place, :]
        b = sine * live_charges[2, place, :] + cosine * live_charges[1, place, :]
        real = a if real is None else real + a
        imaginary = b if imaginary is None else imaginary + b
    values[pl.ds(p, 1), :] = jnp.sum(real, axis=0, keepdims=True)
    values[pl.ds(values.shape[0] // 2 + p, 1), :] = jnp.sum(imaginary, axis=0, keepdims=True)


def ranks(owners):
    blocks = owners.shape[1]
    shape = (blocks, blocks)
    target = jnp.broadcast_to(owners[...].astype(jnp.float32), shape)
    earlier = (target == target.T) & (
        lax.broadcasted_iota(jnp.int32, shape, 0) < lax.broadcasted_iota(jnp.int32, shape, 1)
    )
    return jnp.sum(jnp.where(earlier, 1.0, 0.0), axis=0, keepdims=True)


def fill_slots(values, owners, rank, leaves, sent, capacity):
    devices, _, width = sent.shape
    channels, blocks = values.shape
    device = lax.broadcasted_iota(jnp.int32, (devices, blocks), 0)
    spare = width - capacity * channels
    place_row = lax.broadcasted_iota(jnp.int32, (spare, blocks), 0)
    leaf = jnp.broadcast_to(leaves[...].astype(jnp.float32), (spare, blocks))
    filled = None
    for place in range(capacity):
        pick = jnp.where((device == owners[...]) & (rank == place), 1.0, 0.0).astype(jnp.bfloat16)
        column = jnp.concatenate(
            [
                values[...] if other == place else jnp.zeros((channels, blocks), jnp.float32)
                for other in range(capacity)
            ]
            + [jnp.where(place_row == place, leaf, 0.0)],
            axis=0,
        )
        for term in pieces(column):
            part = lax.dot_general(
                pick, term, (((1,), (1,)), ((), ())), preferred_element_type=jnp.float32
            )
            filled = part if filled is None else filled + part
    sent[:, 0, :] = filled


def raise_part(arrived, upward, capacity, first, count):
    rows = arrived[:, 0, :]
    channels = 2 * count
    values = jnp.concatenate(
        [rows[:, place * channels : (place + 1) * channels] for place in range(capacity)], axis=0
    )
    points = upward.shape[1] // 2
    columns = jnp.concatenate(
        [upward[:, first : first + count], upward[:, points + first : points + first + count]],
        axis=1,
    )
    return lax.dot_general(
        columns,
        values,
        (((1,), (1,)), ((), ())),
        precision=lax.Precision.HIGHEST,
        preferred_element_type=jnp.float32,
    )


def add_up(raised, arrived, capacity, count, leaf_count):
    rows = arrived[:, 0, :]
    first = capacity * 2 * count
    leaf = jnp.concatenate(
        [rows[:, first + place : first + place + 1] for place in range(capacity)], axis=0
    ).astype(jnp.int32)
    members = jnp.where(
        lax.broadcasted_iota(jnp.int32, (leaf.shape[0], leaf_count), 1) == leaf, 1.0, 0.0
    ).astype(jnp.bfloat16)
    summed = sum(
        jnp.dot(term, members, preferred_element_type=jnp.float32) for term in pieces(raised)
    )
    return summed.astype(jnp.bfloat16)


def parents_of(multipole, child_ops):
    channels, leaf_count = multipole.shape
    family = child_ops.shape[1] // channels
    wide = jnp.broadcast_to(
        multipole.astype(jnp.float32)[:, None, :], (channels, family, leaf_count)
    )
    shape = (channels, family, leaf_count)
    mine = lax.broadcasted_iota(jnp.int32, shape, 2) % family == lax.broadcasted_iota(
        jnp.int32, shape, 1
    )
    children = jnp.where(mine, wide, 0.0).reshape(channels * family, leaf_count)
    spread = jnp.dot(
        child_ops[...], children.astype(jnp.bfloat16), preferred_element_type=jnp.float32
    )
    shape = (leaf_count // family, leaf_count)
    group = jnp.where(
        lax.broadcasted_iota(jnp.int32, shape, 1) // family
        == lax.broadcasted_iota(jnp.int32, shape, 0),
        1.0,
        0.0,
    ).astype(jnp.bfloat16)
    return sum(
        lax.dot_general(group, term, (((1,), (1,)), ((), ())), preferred_element_type=jnp.float32)
        for term in pieces(spread)
    )


def step_kernel(
    table,
    positions_in,
    charges_in,
    counts_in,
    owners_in,
    leaves_in,
    near_in,
    image_in,
    upward_in,
    child_in,
    direct_in,
    mirrored_in,
    potentials,
    parents,
    positions,
    charges,
    counts,
    owners,
    leaves,
    lists,
    upward,
    child_ops,
    operators,
    planes,
    depths,
    live_charges,
    early_values,
    late_values,
    early_sent,
    late_sent,
    early_arrived,
    late_arrived,
    windows,
    gathered,
    own_gathered,
    input_sem,
    operator_sem,
    send_sem,
    arrive_sem,
    halo_send,
    halo_recv,
):
    box, depth = lax.axis_index("box"), lax.axis_index("depth")
    boxes, slabs = lax.axis_size("box"), lax.axis_size("depth")
    devices = early_sent.shape[0]
    early, late = early_values.shape[0] // 2, late_values.shape[0] // 2
    channels, leaf_count = potentials.shape
    capacity = early_sent.shape[2] // (2 * early)
    offsets = near_in.shape[0]
    steps, _, width = operators.shape
    batch = width // channels
    half = steps // 2
    me = box * slabs + depth

    fetches = [
        pltpu.make_async_copy(source, place, input_sem.at[number])
        for number, (source, place) in enumerate(
            [
                (positions_in, positions),
                (charges_in, charges),
                (counts_in, counts),
                (owners_in, owners),
                (leaves_in, leaves),
                (near_in, lists.at[pl.ds(0, offsets)]),
                (image_in, lists.at[pl.ds(offsets, offsets)]),
                (upward_in, upward),
                (child_in, child_ops),
            ]
        )
    ]
    for fetch in fetches[:5]:
        fetch.start()
    barrier = pltpu.get_barrier_semaphore()
    columns = [lax.rem(depth + ahead, slabs) for ahead in range(slabs)]

    def own_row(send):
        for column in columns[1:]:
            send(box, column)

    def one_row(ahead, send):
        target_box = lax.rem(box + ahead, boxes)
        for column in columns:
            send(target_box, column)

    def other_rows(send):
        def body(ahead, carry):
            one_row(ahead, send)
            return carry

        lax.fori_loop(1, boxes, body, 0)

    def greet(target_box, target_depth):
        pl.semaphore_signal(
            barrier,
            inc=1,
            device_id=(target_box, target_depth),
            device_id_type=pl.DeviceIdType.MESH,
        )

    own_row(greet)
    other_rows(greet)
    for fetch in fetches[:5]:
        fetch.wait()
    for fetch in fetches[5:]:
        fetch.start()
    for step in range(steps):
        pltpu.make_async_copy(
            (direct_in if step < half else mirrored_in).at[
                :, pl.ds(step % half * width, width)
            ],
            operators.at[step],
            operator_sem.at[step],
        ).start()
    prepare_sources(positions, charges, counts, planes, depths, live_charges)
    rank = ranks(owners)

    def early_point(p, carry):
        sum_point(table, planes, depths, live_charges, early_values, 0, p)
        return carry

    lax.fori_loop(0, early, early_point, 0, unroll=8)
    fill_slots(early_values, owners, rank, leaves, early_sent, capacity)
    pl.semaphore_wait(barrier, devices - 1)

    def route(number, sent, arrived):
        def send(target_box, target_depth):
            pltpu.make_async_remote_copy(
                src_ref=sent.at[target_box * slabs + target_depth],
                dst_ref=arrived.at[me],
                send_sem=send_sem.at[number],
                recv_sem=arrive_sem.at[number],
                device_id=(target_box, target_depth),
                device_id_type=pl.DeviceIdType.MESH,
            ).start()

        return send

    def all_routed(number, sent, arrived):
        others = pl.ds(0, devices - 1)
        return pltpu.make_async_remote_copy(
            src_ref=sent.at[others],
            dst_ref=arrived.at[others],
            send_sem=send_sem.at[number],
            recv_sem=arrive_sem.at[number],
            device_id=(lax.rem(box + 1, boxes), depth),
            device_id_type=pl.DeviceIdType.MESH,
        )

    early_send = route(0, early_sent, early_arrived)
    late_send = route(1, late_sent, late_arrived)
    early_all = all_routed(0, early_sent, early_arrived)
    late_all = all_routed(1, late_sent, late_arrived)
    own_row(early_send)
    one_row(boxes - 1, early_send)

    def late_points(group):
        for p in range(4):
            sum_point(table, planes, depths, live_charges, late_values, early, 4 * group + p)

    def late_and_send(group, carry):
        late_points(group)
        for ahead in range(2):
            one_row(2 * group + 1 + ahead, early_send)
        return carry

    def late_only(group, carry):
        late_points(group)
        return carry

    sending = (boxes - 2) // 2
    lax.fori_loop(0, sending, late_and_send, 0)
    lax.fori_loop(sending, late // 4, late_only, 0)
    fill_slots(late_values, owners, rank, leaves, late_sent, capacity)
    own_row(late_send)
    other_rows(late_send)
    early_arrived[me] = early_sent[me]
    late_arrived[me] = late_sent[me]
    for fetch in fetches[5:]:
        fetch.wait()
    early_all.wait_recv()
    raised = raise_part(early_arrived, upward, capacity, 0, early)
    late_all.wait_recv()
    raised += raise_part(late_arrived, upward, capacity, early, late)
    windows[0, 1] = add_up(raised, late_arrived, capacity, late, leaf_count)

    def copy(number, source, place, device):
        return pltpu.make_async_remote_copy(
            src_ref=windows.at[source],
            dst_ref=windows.at[place],
            send_sem=halo_send.at[number],
            recv_sem=halo_recv.at[number],
            device_id=device,
            device_id_type=pl.DeviceIdType.MESH,
        )

    def beside(number, slab):
        to_right = copy(number, (slab, 1), (slab, 0), (box + 1, depth))
        to_left = copy(number + 1, (slab, 1), (slab, 2), (box - 1, depth))
        return to_right, to_left

    mirror = copy(4, (0, 1), (1, 1), (box, slabs - 1 - depth))
    direct, image = beside(0, 0), beside(2, 1)
    has_left, has_right = box > 0, box < boxes - 1
    blank = jnp.zeros((channels, leaf_count), jnp.bfloat16)

    def start(pair):
        @pl.when(has_right)
        def _():
            pair[0].start()

        @pl.when(has_left)
        def _():
            pair[1].start()

    def receive(pair):
        @pl.when(has_left)
        def _():
            pair[0].wait_recv()

        @pl.when(has_right)
        def _():
            pair[1].wait_recv()

    def sent_off(pair):
        @pl.when(has_right)
        def _():
            pair[0].wait_send()

        @pl.when(has_left)
        def _():
            pair[1].wait_send()

    start(direct)

    @pl.when(jnp.logical_not(has_left))
    def _():
        windows[0, 0] = blank
        windows[1, 0] = blank

    @pl.when(jnp.logical_not(has_right))
    def _():
        windows[0, 2] = blank
        windows[1, 2] = blank

    parents[...] = parents_of(windows[0, 1], child_ops)
    row = lax.broadcasted_iota(jnp.int32, (leaf_count, leaf_count), 0)

    def gather(window, number, parts):
        chosen = lists[number]
        hot = jnp.concatenate(
            [
                jnp.where(row == chosen - part * leaf_count, 1.0, 0.0).astype(jnp.bfloat16)
                for part in parts
            ],
            axis=0,
        )
        return jnp.dot(window, hot, preferred_element_type=jnp.float32).astype(jnp.bfloat16)

    own = windows[0, 1]
    for o in range(batch):
        own_gathered[pl.ds(o * channels, channels), :] = gather(own, o, (1,))
    receive(direct)
    mirror.start()
    beside_own = jnp.concatenate([windows[0, 0], windows[0, 2]], axis=1)
    for o in range(batch):
        place = pl.ds(o * channels, channels)
        gathered[place, :] = own_gathered[place, :] + gather(beside_own, o, (0, 2))
    pltpu.make_async_copy(
        direct_in.at[:, pl.ds(0, width)], operators.at[0], operator_sem.at[0]
    ).wait()
    potentials[...] = jnp.dot(operators[0], gathered[...], preferred_element_type=jnp.float32)

    def translate(step, carry):
        @pl.when(step == half // 2)
        def _():
            mirror.wait_recv()
            start(image)

        @pl.when(step == half)
        def _():
            receive(image)

        pltpu.make_async_copy(
            direct_in.at[:, pl.ds(0, width)], operators.at[step], operator_sem.at[step]
        ).wait()
        slab = step // half
        window = jnp.concatenate([windows[slab, part] for part in range(3)], axis=1)
        for o in range(batch):
            gathered[pl.ds(o * channels, channels), :] = gather(
                window, step * batch + o, (0, 1, 2)
            )
        potentials[...] += jnp.dot(
            operators[step], gathered[...], preferred_element_type=jnp.float32
        )
        return carry

    lax.fori_loop(1, steps, translate, 0)
    early_all.wait_send()
    late_all.wait_send()
    sent_off(direct)
    sent_off(image)
    mirror.wait_send()


def hand_over_kernel(potentials, parents, potentials_out, parents_out):
    potentials_out[:, 0, :] = potentials[...]
    parents_out[...] = parents[...]


def local(
    positions,
    charges,
    counts,
    owners,
    leaves,
    near_lists,
    image_lists,
    upward,
    child_ops,
    direct_ops,
    image_ops,
):
    devices = lax.axis_size("box") * lax.axis_size("depth")
    blocks, rows = positions.shape[1:]
    capacity = 2 * blocks // devices
    offsets, _, leaf_count = near_lists.shape
    channels = upward.shape[0]
    index = surface_index(GRID)
    table = jnp.asarray(np.stack([index[:, 0] * GRID + index[:, 1], index[:, 2]]))
    batch = 32
    steps = 2 * offsets // batch
    points = channels // 2
    early = points * 11 // 16 // 8 * 8
    parts = (early, points - early)
    widths = [-(-capacity * (2 * part + 1) // 128) * 128 for part in parts]
    parent_count = leaf_count * channels // child_ops.shape[1]

    def scratch(*shape, dtype=jnp.float32):
        return pltpu.VMEM(shape, dtype)

    potentials, parents = pl.pallas_call(
        step_kernel,
        out_shape=(
            jax.ShapeDtypeStruct((channels, leaf_count), jnp.float32),
            jax.ShapeDtypeStruct((parent_count, channels), jnp.float32),
        ),
        in_specs=[SM] + [HBM] * 11,
        out_specs=(VM, VM),
        scratch_shapes=[
            scratch(*positions.shape),
            scratch(*charges.shape),
            scratch(1, blocks, dtype=jnp.int32),
            scratch(1, blocks, dtype=jnp.int32),
            scratch(1, blocks, dtype=jnp.int32),
            scratch(2 * offsets, 1, leaf_count, dtype=jnp.int32),
            scratch(*upward.shape),
            scratch(*child_ops.shape, dtype=jnp.bfloat16),
            scratch(steps, channels, batch * channels, dtype=jnp.bfloat16),
            scratch(GRID * GRID, rows, blocks),
            scratch(GRID, rows, blocks),
            scratch(4, rows, blocks),
            *[scratch(2 * part, blocks) for part in parts],
            *[scratch(devices, 1, width) for width in widths * 2],
            scratch(2, 3, channels, leaf_count, dtype=jnp.bfloat16),
            scratch(batch * channels, leaf_count, dtype=jnp.bfloat16),
            scratch(batch * channels, leaf_count, dtype=jnp.bfloat16),
            pltpu.SemaphoreType.DMA((9,)),
            pltpu.SemaphoreType.DMA((steps,)),
            pltpu.SemaphoreType.DMA((2,)),
            pltpu.SemaphoreType.DMA((2,)),
            pltpu.SemaphoreType.DMA((5,)),
            pltpu.SemaphoreType.DMA((5,)),
        ],
        compiler_params=pltpu.CompilerParams(
            vmem_limit_bytes=56 << 20, has_side_effects=True, collective_id=0
        ),
        name="step",
    )(
        table,
        positions,
        charges,
        counts.reshape(1, blocks),
        owners.reshape(1, blocks),
        leaves.reshape(1, blocks),
        near_lists,
        image_lists,
        upward,
        child_ops,
        direct_ops.T,
        image_ops.T,
    )
    potentials, parents = pl.pallas_call(
        hand_over_kernel,
        out_shape=(
            jax.ShapeDtypeStruct((channels, 1, leaf_count), jnp.float32),
            jax.ShapeDtypeStruct((parent_count, channels), jnp.float32),
        ),
        in_specs=[VM, VM],
        out_specs=(VM, VM),
        name="hand_over",
    )(potentials, parents)
    return (potentials, parents.T[:, None, :])


def solution(mesh):
    return jax.shard_map(
        local,
        mesh=mesh,
        in_specs=(
            P(None, ("box", "depth"), None),
            P(None, ("box", "depth"), None),
            P(("box", "depth")),
            P(("box", "depth"), None),
            P(("box", "depth")),
            P(None, "depth", "box"),
            P(None, "depth", "box"),
            P(),
            P(),
            P(),
            P(),
        ),
        out_specs=(P(None, "depth", "box"), P(None, "depth", "box")),
        check_vma=False,
    )
```

```python
import functools

import jax
import jax.numpy as jnp
import numpy as np
from jax import lax
from jax.experimental import pallas as pl
from jax.experimental.pallas import tpu as pltpu
from jax.sharding import PartitionSpec as P
from numpy.polynomial import chebyshev, polynomial

GRID = 6
VM = pl.BlockSpec(memory_space=pltpu.VMEM)
HBM = pl.BlockSpec(memory_space=pltpu.HBM)
SM = pl.BlockSpec(memory_space=pltpu.SMEM)


def surface_index(grid_size):
    indices = np.arange(grid_size)
    lattice = np.stack(np.meshgrid(indices, indices, indices, indexing="ij"), -1).reshape(-1, 3)
    outside = np.any((lattice == 0) | (lattice == grid_size - 1), axis=1)
    return lattice[outside].astype(np.int32)


def node_coordinates(grid_size):
    middle = (grid_size - 1) / 2.0
    return ((np.arange(grid_size) - middle) * (1.5 / middle)).astype(np.float32)


def series(function, degree):
    fitted = chebyshev.Chebyshev.interpolate(function, degree, domain=[1.0, 12.0])
    return [float(value) for value in fitted.convert(kind=polynomial.Polynomial).coef]


HALF_SINE = series(lambda s: np.sin(np.sqrt(s) / 2) / (np.sqrt(s) / 2), 4)
HALF_COSINE = series(lambda s: np.cos(np.sqrt(s) / 2), 5)


SCALE = 2.0 * HALF_SINE[-1] * HALF_COSINE[-1]


def monic(coefficients, s):
    value = s + coefficients[-2] / coefficients[-1]
    for coefficient in coefficients[-3::-1]:
        value = value * s + coefficient / coefficients[-1]
    return value


def waves(s):
    sine = monic(HALF_SINE, s)
    cosine = monic(HALF_COSINE, s)
    sine = sine * cosine
    cosine = cosine * cosine * (2.0 * HALF_COSINE[-1] ** 2) - 1.0
    return (cosine * cosine - 0.5) * lax.rsqrt(s), sine * cosine


def pieces(value, count=3):
    terms = []
    for _ in range(count):
        terms.append(value.astype(jnp.bfloat16))
        value = value - terms[-1].astype(jnp.float32)
    return terms


def prepare_sources(positions, charges, counts, planes, depths, live_charges):
    nodes = node_coordinates(GRID)
    blocks, rows = positions.shape[1:]
    x, y, z = positions[0].T, positions[1].T, positions[2].T
    squares = []
    for node in nodes:
        delta = float(node) - y
        squares.append(delta * delta)
    for i, node in enumerate(nodes):
        delta = float(node) - x
        delta = delta * delta
        for j in range(len(nodes)):
            planes[i * len(nodes) + j] = delta + squares[j]
        delta = float(node) - z
        depths[i] = delta * delta
    live = lax.broadcasted_iota(jnp.int32, (rows, blocks), 0) < counts[...]
    for part in range(2):
        charge = jnp.where(live, charges[part].T, 0.0)
        live_charges[part] = 2.0 * charge
        live_charges[2 + part] = SCALE * charge


def sum_point(table, planes, depths, live_charges, values, first, p):
    plane = table[0, first + p]
    depth = table[1, first + p]
    real = imaginary = None
    for chunk in range(planes.shape[1] // 8):
        place = pl.ds(8 * chunk, 8)
        cosine, sine = waves(planes[plane, place, :] + depths[depth, place, :])
        a = cosine * live_charges[0, place, :] - sine * live_charges[3, place, :]
        b = sine * live_charges[2, place, :] + cosine * live_charges[1, place, :]
        real = a if real is None else real + a
        imaginary = b if imaginary is None else imaginary + b
    values[pl.ds(p, 1), :] = jnp.sum(real, axis=0, keepdims=True)
    values[pl.ds(values.shape[0] // 2 + p, 1), :] = jnp.sum(imaginary, axis=0, keepdims=True)


def ranks(owners):
    blocks = owners.shape[1]
    shape = (blocks, blocks)
    target = jnp.broadcast_to(owners[...].astype(jnp.float32), shape)
    earlier = (target == target.T) & (
        lax.broadcasted_iota(jnp.int32, shape, 0) < lax.broadcasted_iota(jnp.int32, shape, 1)
    )
    return jnp.sum(jnp.where(earlier, 1.0, 0.0), axis=0, keepdims=True)


def fill_slots(values, owners, rank, leaves, sent, capacity):
    devices, _, width = sent.shape
    channels, blocks = values.shape
    device = lax.broadcasted_iota(jnp.int32, (devices, blocks), 0)
    spare = width - capacity * channels
    place_row = lax.broadcasted_iota(jnp.int32, (spare, blocks), 0)
    leaf = jnp.broadcast_to(leaves[...].astype(jnp.float32), (spare, blocks))
    filled = None
    for place in range(capacity):
        pick = jnp.where((device == owners[...]) & (rank == place), 1.0, 0.0).astype(jnp.bfloat16)
        column = jnp.concatenate(
            [
                values[...] if other == place else jnp.zeros((channels, blocks), jnp.float32)
                for other in range(capacity)
            ]
            + [jnp.where(place_row == place, leaf, 0.0)],
            axis=0,
        )
        for term in pieces(column):
            part = lax.dot_general(
                pick, term, (((1,), (1,)), ((), ())), preferred_element_type=jnp.float32
            )
            filled = part if filled is None else filled + part
    sent[:, 0, :] = filled


def raise_part(arrived, upward, capacity, first, count):
    rows = arrived[:, 0, :]
    channels = 2 * count
    values = jnp.concatenate(
        [rows[:, place * channels : (place + 1) * channels] for place in range(capacity)], axis=0
    )
    points = upward.shape[1] // 2
    columns = jnp.concatenate(
        [upward[:, first : first + count], upward[:, points + first : points + first + count]],
        axis=1,
    )
    return lax.dot_general(
        columns,
        values,
        (((1,), (1,)), ((), ())),
        precision=lax.Precision.HIGHEST,
        preferred_element_type=jnp.float32,
    )


def add_up(raised, arrived, capacity, count, leaf_count):
    rows = arrived[:, 0, :]
    first = capacity * 2 * count
    leaf = jnp.concatenate(
        [rows[:, first + place : first + place + 1] for place in range(capacity)], axis=0
    ).astype(jnp.int32)
    members = jnp.where(
        lax.broadcasted_iota(jnp.int32, (leaf.shape[0], leaf_count), 1) == leaf, 1.0, 0.0
    ).astype(jnp.bfloat16)
    summed = sum(
        jnp.dot(term, members, preferred_element_type=jnp.float32) for term in pieces(raised)
    )
    return summed.astype(jnp.bfloat16)


def parents_of(multipole, child_ops):
    channels, leaf_count = multipole.shape
    family = child_ops.shape[1] // channels
    wide = jnp.broadcast_to(
        multipole.astype(jnp.float32)[:, None, :], (channels, family, leaf_count)
    )
    shape = (channels, family, leaf_count)
    mine = lax.broadcasted_iota(jnp.int32, shape, 2) % family == lax.broadcasted_iota(
        jnp.int32, shape, 1
    )
    children = jnp.where(mine, wide, 0.0).reshape(channels * family, leaf_count)
    spread = jnp.dot(
        child_ops[...], children.astype(jnp.bfloat16), preferred_element_type=jnp.float32
    )
    shape = (leaf_count // family, leaf_count)
    group = jnp.where(
        lax.broadcasted_iota(jnp.int32, shape, 1) // family
        == lax.broadcasted_iota(jnp.int32, shape, 0),
        1.0,
        0.0,
    ).astype(jnp.bfloat16)
    return sum(
        lax.dot_general(group, term, (((1,), (1,)), ((), ())), preferred_element_type=jnp.float32)
        for term in pieces(spread)
    )


def step_kernel(
    table,
    positions_in,
    charges_in,
    counts_in,
    owners_in,
    leaves_in,
    near_in,
    image_in,
    upward_in,
    child_in,
    direct_in,
    mirrored_in,
    potentials,
    parents,
    positions,
    charges,
    counts,
    owners,
    leaves,
    lists,
    upward,
    child_ops,
    operators,
    planes,
    depths,
    live_charges,
    early_values,
    late_values,
    early_sent,
    late_sent,
    early_arrived,
    late_arrived,
    windows,
    gathered,
    own_gathered,
    input_sem,
    operator_sem,
    send_sem,
    arrive_sem,
    halo_send,
    halo_recv,
):
    box, depth = lax.axis_index("box"), lax.axis_index("depth")
    boxes, slabs = lax.axis_size("box"), lax.axis_size("depth")
    devices = early_sent.shape[0]
    early, late = early_values.shape[0] // 2, late_values.shape[0] // 2
    channels, leaf_count = potentials.shape
    capacity = early_sent.shape[2] // (2 * early)
    offsets = near_in.shape[0]
    steps, _, width = operators.shape
    batch = width // channels
    half = steps // 2
    me = box * slabs + depth

    fetches = [
        pltpu.make_async_copy(source, place, input_sem.at[number])
        for number, (source, place) in enumerate(
            [
                (positions_in, positions),
                (charges_in, charges),
                (counts_in, counts),
                (owners_in, owners),
                (leaves_in, leaves),
                (near_in, lists.at[pl.ds(0, offsets)]),
                (image_in, lists.at[pl.ds(offsets, offsets)]),
                (upward_in, upward),
                (child_in, child_ops),
            ]
        )
    ]
    for fetch in fetches[:5]:
        fetch.start()
    barrier = pltpu.get_barrier_semaphore()
    columns = [lax.rem(depth + ahead, slabs) for ahead in range(slabs)]

    def own_row(send):
        for column in columns[1:]:
            send(box, column)

    def one_row(ahead, send):
        target_box = lax.rem(box + ahead, boxes)
        for column in columns:
            send(target_box, column)

    def other_rows(send):
        def body(ahead, carry):
            one_row(ahead, send)
            return carry

        lax.fori_loop(1, boxes, body, 0)

    def greet(target_box, target_depth):
        pl.semaphore_signal(
            barrier,
            inc=1,
            device_id=(target_box, target_depth),
            device_id_type=pl.DeviceIdType.MESH,
        )

    own_row(greet)
    other_rows(greet)
    for fetch in fetches[:5]:
        fetch.wait()
    for fetch in fetches[5:]:
        fetch.start()
    for step in range(steps):
        pltpu.make_async_copy(
            (direct_in if step < half else mirrored_in).at[
                :, pl.ds(step % half * width, width)
            ],
            operators.at[step],
            operator_sem.at[step],
        ).start()
    prepare_sources(positions, charges, counts, planes, depths, live_charges)
    rank = ranks(owners)

    def early_point(p, carry):
        sum_point(table, planes, depths, live_charges, early_values, 0, p)
        return carry

    lax.fori_loop(0, early, early_point, 0, unroll=8)
    fill_slots(early_values, owners, rank, leaves, early_sent, capacity)
    pl.semaphore_wait(barrier, devices - 1)

    def route(number, sent, arrived):
        def send(target_box, target_depth):
            pltpu.make_async_remote_copy(
                src_ref=sent.at[target_box * slabs + target_depth],
                dst_ref=arrived.at[me],
                send_sem=send_sem.at[number],
                recv_sem=arrive_sem.at[number],
                device_id=(target_box, target_depth),
                device_id_type=pl.DeviceIdType.MESH,
            ).start()

        return send

    def all_routed(number, sent, arrived):
        others = pl.ds(0, devices - 1)
        return pltpu.make_async_remote_copy(
            src_ref=sent.at[others],
            dst_ref=arrived.at[others],
            send_sem=send_sem.at[number],
            recv_sem=arrive_sem.at[number],
            device_id=(lax.rem(box + 1, boxes), depth),
            device_id_type=pl.DeviceIdType.MESH,
        )

    early_send = route(0, early_sent, early_arrived)
    late_send = route(1, late_sent, late_arrived)
    early_all = all_routed(0, early_sent, early_arrived)
    late_all = all_routed(1, late_sent, late_arrived)
    own_row(early_send)
    one_row(boxes - 1, early_send)

    def late_points(group):
        for p in range(4):
            sum_point(table, planes, depths, live_charges, late_values, early, 4 * group + p)

    def late_and_send(group, carry):
        late_points(group)
        for ahead in range(2):
            one_row(2 * group + 1 + ahead, early_send)
        return carry

    def late_only(group, carry):
        late_points(group)
        return carry

    sending = (boxes - 2) // 2
    lax.fori_loop(0, sending, late_and_send, 0)
    lax.fori_loop(sending, late // 4, late_only, 0)
    fill_slots(late_values, owners, rank, leaves, late_sent, capacity)
    own_row(late_send)
    other_rows(late_send)
    early_arrived[me] = early_sent[me]
    late_arrived[me] = late_sent[me]
    for fetch in fetches[5:]:
        fetch.wait()
    early_all.wait_recv()
    raised = raise_part(early_arrived, upward, capacity, 0, early)
    late_all.wait_recv()
    raised += raise_part(late_arrived, upward, capacity, early, late)
    windows[0, 1] = add_up(raised, late_arrived, capacity, late, leaf_count)

    def copy(number, source, place, device):
        return pltpu.make_async_remote_copy(
            src_ref=windows.at[source],
            dst_ref=windows.at[place],
            send_sem=halo_send.at[number],
            recv_sem=halo_recv.at[number],
            device_id=device,
            device_id_type=pl.DeviceIdType.MESH,
        )

    def beside(number, slab):
        to_right = copy(number, (slab, 1), (slab, 0), (box + 1, depth))
        to_left = copy(number + 1, (slab, 1), (slab, 2), (box - 1, depth))
        return to_right, to_left

    mirror = copy(4, (0, 1), (1, 1), (box, slabs - 1 - depth))
    direct, image = beside(0, 0), beside(2, 1)
    has_left, has_right = box > 0, box < boxes - 1
    blank = jnp.zeros((channels, leaf_count), jnp.bfloat16)

    def start(pair):
        @pl.when(has_right)
        def _():
            pair[0].start()

        @pl.when(has_left)
        def _():
            pair[1].start()

    def receive(pair):
        @pl.when(has_left)
        def _():
            pair[0].wait_recv()

        @pl.when(has_right)
        def _():
            pair[1].wait_recv()

    def sent_off(pair):
        @pl.when(has_right)
        def _():
            pair[0].wait_send()

        @pl.when(has_left)
        def _():
            pair[1].wait_send()

    start(direct)

    @pl.when(jnp.logical_not(has_left))
    def _():
        windows[0, 0] = blank
        windows[1, 0] = blank

    @pl.when(jnp.logical_not(has_right))
    def _():
        windows[0, 2] = blank
        windows[1, 2] = blank

    parents[...] = parents_of(windows[0, 1], child_ops)
    row = lax.broadcasted_iota(jnp.int32, (leaf_count, leaf_count), 0)
    row = row.astype(jnp.float32).astype(jnp.bfloat16)
    hit, miss = jnp.ones((), jnp.bfloat16), jnp.zeros((), jnp.bfloat16)

    def gather(window, number, parts):
        chosen = lists[number].astype(jnp.float32)
        hot = jnp.concatenate(
            [
                jnp.where(row == (chosen - float(part * leaf_count)).astype(jnp.bfloat16), hit, miss)
                for part in parts
            ],
            axis=0,
        )
        return jnp.dot(window, hot, preferred_element_type=jnp.float32).astype(jnp.bfloat16)

    own = windows[0, 1]
    for o in range(batch):
        own_gathered[pl.ds(o * channels, channels), :] = gather(own, o, (1,))
    receive(direct)
    mirror.start()
    beside_own = jnp.concatenate([windows[0, 0], windows[0, 2]], axis=1)
    for o in range(batch):
        place = pl.ds(o * channels, channels)
        gathered[place, :] = own_gathered[place, :] + gather(beside_own, o, (0, 2))
    pltpu.make_async_copy(
        direct_in.at[:, pl.ds(0, width)], operators.at[0], operator_sem.at[0]
    ).wait()
    potentials[...] = jnp.dot(operators[0], gathered[...], preferred_element_type=jnp.float32)

    def translate(step, carry):
        @pl.when(step == half // 2)
        def _():
            mirror.wait_recv()
            start(image)

        @pl.when(step == half)
        def _():
            receive(image)

        pltpu.make_async_copy(
            direct_in.at[:, pl.ds(0, width)], operators.at[step], operator_sem.at[step]
        ).wait()
        slab = step // half
        window = jnp.concatenate([windows[slab, part] for part in range(3)], axis=1)
        for o in range(batch):
            gathered[pl.ds(o * channels, channels), :] = gather(
                window, step * batch + o, (0, 1, 2)
            )
        potentials[...] += jnp.dot(
            operators[step], gathered[...], preferred_element_type=jnp.float32
        )
        return carry

    lax.fori_loop(1, steps, translate, 0)
    early_all.wait_send()
    late_all.wait_send()
    sent_off(direct)
    sent_off(image)
    mirror.wait_send()


def hand_over_kernel(potentials, parents, potentials_out, parents_out):
    potentials_out[:, 0, :] = potentials[...]
    parents_out[...] = parents[...]


def local(
    positions,
    charges,
    counts,
    owners,
    leaves,
    near_lists,
    image_lists,
    upward,
    child_ops,
    direct_ops,
    image_ops,
):
    devices = lax.axis_size("box") * lax.axis_size("depth")
    blocks, rows = positions.shape[1:]
    capacity = 2 * blocks // devices
    offsets, _, leaf_count = near_lists.shape
    channels = upward.shape[0]
    index = surface_index(GRID)
    table = jnp.asarray(np.stack([index[:, 0] * GRID + index[:, 1], index[:, 2]]))
    batch = 32
    steps = 2 * offsets // batch
    points = channels // 2
    early = points * 13 // 16 // 8 * 8
    parts = (early, points - early)
    widths = [-(-capacity * (2 * part + 1) // 128) * 128 for part in parts]
    parent_count = leaf_count * channels // child_ops.shape[1]

    def scratch(*shape, dtype=jnp.float32):
        return pltpu.VMEM(shape, dtype)

    potentials, parents = pl.pallas_call(
        step_kernel,
        out_shape=(
            jax.ShapeDtypeStruct((channels, leaf_count), jnp.float32),
            jax.ShapeDtypeStruct((parent_count, channels), jnp.float32),
        ),
        in_specs=[SM] + [HBM] * 11,
        out_specs=(VM, VM),
        scratch_shapes=[
            scratch(*positions.shape),
            scratch(*charges.shape),
            scratch(1, blocks, dtype=jnp.int32),
            scratch(1, blocks, dtype=jnp.int32),
            scratch(1, blocks, dtype=jnp.int32),
            scratch(2 * offsets, 1, leaf_count, dtype=jnp.int32),
            scratch(*upward.shape),
            scratch(*child_ops.shape, dtype=jnp.bfloat16),
            scratch(steps, channels, batch * channels, dtype=jnp.bfloat16),
            scratch(GRID * GRID, rows, blocks),
            scratch(GRID, rows, blocks),
            scratch(4, rows, blocks),
            *[scratch(2 * part, blocks) for part in parts],
            *[scratch(devices, 1, width) for width in widths * 2],
            scratch(2, 3, channels, leaf_count, dtype=jnp.bfloat16),
            scratch(batch * channels, leaf_count, dtype=jnp.bfloat16),
            scratch(batch * channels, leaf_count, dtype=jnp.bfloat16),
            pltpu.SemaphoreType.DMA((9,)),
            pltpu.SemaphoreType.DMA((steps,)),
            pltpu.SemaphoreType.DMA((2,)),
            pltpu.SemaphoreType.DMA((2,)),
            pltpu.SemaphoreType.DMA((5,)),
            pltpu.SemaphoreType.DMA((5,)),
        ],
        compiler_params=pltpu.CompilerParams(
            vmem_limit_bytes=56 << 20, has_side_effects=True, collective_id=0
        ),
        name="step",
    )(
        table,
        positions,
        charges,
        counts.reshape(1, blocks),
        owners.reshape(1, blocks),
        leaves.reshape(1, blocks),
        near_lists,
        image_lists,
        upward,
        child_ops,
        direct_ops.T,
        image_ops.T,
    )
    potentials, parents = pl.pallas_call(
        hand_over_kernel,
        out_shape=(
            jax.ShapeDtypeStruct((channels, 1, leaf_count), jnp.float32),
            jax.ShapeDtypeStruct((parent_count, channels), jnp.float32),
        ),
        in_specs=[VM, VM],
        out_specs=(VM, VM),
        name="hand_over",
    )(potentials, parents)
    return (potentials, parents.T[:, None, :])


def solution(mesh):
    return jax.shard_map(
        local,
        mesh=mesh,
        in_specs=(
            P(None, ("box", "depth"), None),
            P(None, ("box", "depth"), None),
            P(("box", "depth")),
            P(("box", "depth"), None),
            P(("box", "depth")),
            P(None, "depth", "box"),
            P(None, "depth", "box"),
            P(),
            P(),
            P(),
            P(),
        ),
        out_specs=(P(None, "depth", "box"), P(None, "depth", "box")),
        check_vma=False,
    )
```
